256 devices in a mesh: tile: 32 (over x, z), ens: 8 (over y, core).
Axes of the slice: x: 4, y: 4, z: 8, core: 2. Of those that a mesh axis runs over, the one named last changes fastest.
Arguments:
- initial_sample_set: float32 [80, 2, 128, 2048], P('ens', None, 'tile'), may hold values from -6 to 6
- flow_velocity: float32 [2, 2, 128, 2048], P(None, None, 'tile'), may hold values from -0.4 to 0.4
- obs_loc: int32 [3, 2, 32768], P(None, None, 'tile'), may hold values from 0 to 2047, as said below
- obs_count: int32 [2, 32], P(None, 'tile'), may hold values from 256 to 1024, as said below
- obs_value: float32 [2, 32768], P(None, 'tile'), may hold values from -6 to 6
- obs_error: float32 [2, 32768], P(None, 'tile'), may hold values from 0.25 to 2
Outputs:
- analysis: float32 [80, 2, 128, 2048], P('ens', None, 'tile')
The draws below stay inside these ranges and needn't reach their ends.
Inputs may be any that keep to these rules, and one draw needn't show every extreme that they name: `obs_loc`: slots 1024 * t to 1024 * (t + 1) - 1 of a batch belong to tile t: their row lies in rows 4 * t to 4 * (t + 1) - 1; columns lie in 0 to 2047 and levels in 0 to 1. `obs_count`: in every batch some tile has exactly 1024 live observations; a tile's live observations are its first slots.
All inputs are finite; a program needn't handle non-finite values.
Results may differ from the reference program's by a relative error of at most 0.0003.
Values sent between devices are 32-bit elements; how exact they have to be, the bound alone decides.
A program may use at most 128 MiB of HBM per device.

```python
import math
import jax
import jax.numpy as jnp
from jax import lax

MEMBERS = 80
LEVELS = 2
ROWS_DEV = 4
NY = 2048
OBS_TILE = 1024
BATCHES = 2
REACH = 2
TILES = 32
NX = 128
OBS = 32768


def draw_obs_count(key, part):
    random_seed_input = jax.random.fold_in(key, 31)
    key_full = jax.random.fold_in(key, 57)
    fewest = OBS_TILE // 4
    span_count = OBS_TILE - fewest + 1
    draws_load = jax.random.randint(random_seed_input, (BATCHES, TILES), 0, span_count)
    counts = fewest + draws_load * draws_load // span_count
    busiest = jax.random.randint(key_full, (BATCHES, 1), 0, TILES)
    tile_numbers = jnp.arange(TILES)[None, :]
    return jnp.where(tile_numbers == busiest, OBS_TILE, counts).astype(jnp.int32)


def draw_obs_loc(key, part):
    owner = jnp.arange(OBS) // OBS_TILE
    row_inside = jax.random.randint(jax.random.fold_in(key, 71), (BATCHES, OBS), 0, ROWS_DEV)
    column = jax.random.randint(jax.random.fold_in(key, 72), (BATCHES, OBS), 0, NY)
    levels_drawn = jax.random.randint(jax.random.fold_in(key, 73), (BATCHES, OBS), 0, LEVELS)
    row_inside = row_inside.at[:, 0].set(0)
    row_inside = row_inside.at[:, OBS - 1].set(ROWS_DEV - 1)
    column = column.at[:, 0].set(NY - 1)
    column = column.at[:, 1].set(0)
    rows_drawn = owner[None, :] * ROWS_DEV + row_inside
    return jnp.stack([rows_drawn, column, levels_drawn]).astype(jnp.int32)


def block_scale(stream_key, shape, pieces, least, top_value):
    level = 1.0
    for dim, parts in pieces:
        heights = jax.random.uniform(jax.random.fold_in(jax.random.fold_in(stream_key, 6), dim), (parts,), jnp.float32, least / len(pieces), top_value / len(pieces))
        level = level * jnp.repeat(jnp.exp(heights), shape[dim] // parts).reshape((-1,) + (1,) * (len(shape) - 1 - dim))
    return level


def scatter_about(stream_key, dims, width, limit, shards=(), held_as=jnp.bfloat16):
    values = width * jax.random.normal(stream_key, dims, jnp.float32)
    if shards:
        values = values * block_scale(stream_key, dims, shards, -0.22, 0.18)
    return jnp.clip(values, -limit, limit).astype(held_as)


def setup_inputs(seed: int = 0) -> dict:
    keys = jax.random.split(jax.random.key(seed), 7)
    return {
        "initial_sample_set": scatter_about(keys[0], (MEMBERS, LEVELS, NX, NY), 1.0, 6.0, ((0, 8), (2, 32)), jnp.float32),
        "flow_velocity": jnp.clip(jax.random.uniform(keys[1], (2, LEVELS, NX, NY), jnp.float32, -0.4, 0.4) * block_scale(keys[1], (2, LEVELS, NX, NY), ((2, 32),), -0.4, 0.0), -0.4, 0.4),
        "obs_loc": draw_obs_loc(jax.random.fold_in(keys[6], 71), 0),
        "obs_count": draw_obs_count(jax.random.fold_in(keys[6], 71), 0),
        "obs_value": scatter_about(keys[4], (BATCHES, OBS), 1.0, 6.0, ((1, 32),), jnp.float32),
        "obs_error": jnp.clip(jnp.exp(math.log(2.0) - 2.0794415 * jax.random.uniform(keys[5], (BATCHES, OBS), jnp.float32) ** block_scale(keys[5], (BATCHES, OBS), ((1, 32),), -0.2, 0.2)), 0.25, 2.0),
    }


SPREAD_RATE = 0.05
EPSILON = 1e-06
PRECISE = lax.Precision.HIGHEST

def advance(centre, row_above, row_below, col_left, col_right, flow_velocity):
    wind_rows = flow_velocity[0][None]
    wind_cols = flow_velocity[1][None]
    tendency = jnp.maximum(wind_rows, 0.0) * (centre - row_above) + jnp.minimum(wind_rows, 0.0) * (row_below - centre) + jnp.maximum(wind_cols, 0.0) * (centre - col_left) + jnp.minimum(wind_cols, 0.0) * (col_right - centre)
    return centre - tendency + SPREAD_RATE * (row_above + row_below + col_left + col_right - 4.0 * centre)

def increments(prior_obs, row_values, error_row, live_mask):
    members = prior_obs.shape[0]
    average = lax.optimization_barrier(jnp.sum(prior_obs, axis=0)) / members
    deviation = prior_obs - average[None, :]
    var_prior = lax.optimization_barrier(jnp.sum(deviation * deviation, axis=0)) / (members - 1) + EPSILON
    combined = var_prior + error_row
    shrink_factor = jnp.sqrt(error_row / combined)
    mean_post = (error_row * average + var_prior * row_values) / combined
    obs_shift = live_mask[None, :] * ((shrink_factor - 1.0)[None, :] * deviation + (mean_post - average)[None, :])
    weight = live_mask[None, :] * deviation / ((members - 1) * var_prior)[None, :]
    return (weight, obs_shift)

def block_gain(states, weight, obs_shift, obs_place, cell_lev, cell_row, cell_col, radius, col_radius):
    covariance = lax.dot_general(weight, states, (((0,), (0,)), ((), ())), precision=PRECISE, preferred_element_type=jnp.float32)
    row_gap = cell_row[None, :] - obs_place[0][:, None]
    column_spacing = cell_col[None, :] - obs_place[1][:, None]
    level_gap = jnp.abs(cell_lev[None, :] - obs_place[2][:, None])
    closeness = jnp.maximum(1.0 - row_gap * row_gap / (radius * radius) - column_spacing * column_spacing / (col_radius * col_radius), 0.0)
    gain_map = covariance * (closeness * closeness / (1.0 + level_gap))
    return jnp.dot(obs_shift, gain_map, precision=PRECISE, preferred_element_type=jnp.float32)

def reference(initial_sample_set, flow_velocity, obs_loc, obs_count, obs_value, obs_error):
    padded = jnp.pad(initial_sample_set, ((0, 0), (0, 0), (1, 1), (1, 1)))
    current_model_vector = advance(padded[:, :, 1:-1, 1:-1], padded[:, :, :-2, 1:-1], padded[:, :, 2:, 1:-1], padded[:, :, 1:-1, :-2], padded[:, :, 1:-1, 2:], flow_velocity)
    members, levels, row_total, col_total = current_model_vector.shape
    obs_total = obs_value.shape[1]
    slots = jnp.arange(obs_total, dtype=jnp.int32)
    owners = slots // OBS_TILE
    window = 2 * REACH + 1
    radius = float(REACH * ROWS_DEV)
    col_radius = float(col_total // 2)
    cell_index = jnp.arange(levels * ROWS_DEV * col_total, dtype=jnp.int32)
    cell_lev = (cell_index // (ROWS_DEV * col_total)).astype(jnp.float32)
    local_row = cell_index // col_total % ROWS_DEV
    cell_col = (cell_index % col_total).astype(jnp.float32)
    for batch_index in range(BATCHES):
        rows_obs = obs_loc[0, batch_index]
        cols_obs = obs_loc[1, batch_index]
        levs_obs = obs_loc[2, batch_index]
        flat_state = current_model_vector.reshape(members, -1)
        prior_obs = jnp.take(flat_state, (levs_obs * row_total + rows_obs) * col_total + cols_obs, axis=1)
        live_mask = (slots % OBS_TILE < obs_count[batch_index][owners]).astype(jnp.float32)
        weight, obs_shift = increments(prior_obs, obs_value[batch_index], obs_error[batch_index], live_mask)
        obs_place = obs_loc[:, batch_index].astype(jnp.float32)
        border = ((0, 0), (REACH, REACH), (0, 0))
        weight_pad = jnp.pad(weight.reshape(members, TILES, OBS_TILE), border)
        shift_pad = jnp.pad(obs_shift.reshape(members, TILES, OBS_TILE), border)
        place_pad = jnp.pad(obs_place.reshape(3, TILES, OBS_TILE), border)

        def count_per_tile(tile_index, current_grid_array=current_model_vector, weight_pad=weight_pad, shift_pad=shift_pad, place_pad=place_pad):
            near_weight = lax.dynamic_slice_in_dim(weight_pad, tile_index, window, 1).reshape(members, window * OBS_TILE)
            near_shift = lax.dynamic_slice_in_dim(shift_pad, tile_index, window, 1).reshape(members, window * OBS_TILE)
            near_place = lax.dynamic_slice_in_dim(place_pad, tile_index, window, 1).reshape(3, window * OBS_TILE)
            cells = lax.dynamic_slice_in_dim(current_grid_array, tile_index * ROWS_DEV, ROWS_DEV, 2).reshape(members, -1)
            cell_row = (tile_index * ROWS_DEV + local_row).astype(jnp.float32)
            update = block_gain(cells, near_weight, near_shift, near_place, cell_lev, cell_row, cell_col, radius, col_radius)
            return update.reshape(members, levels, ROWS_DEV, col_total)
        updates = lax.map(count_per_tile, jnp.arange(TILES, dtype=jnp.int32))
        current_model_vector = current_model_vector + jnp.transpose(updates, (1, 2, 0, 3, 4)).reshape(current_model_vector.shape)
    return current_model_vector
```

```python
import functools

import jax
import jax.numpy as jnp
from jax import lax
from jax.experimental import pallas as pl
from jax.experimental.pallas import tpu as pltpu
from jax.sharding import PartitionSpec as P

BATCHES = 2
REACH = 2
WINDOW = 2 * REACH + 1
SPREAD_RATE = 0.05
EPSILON = 1e-06
MESH = pl.DeviceIdType.MESH
VMEM = pltpu.VMEM
LANES = 128
BLOCK = 256
FORWARD_RIGHT = (2, 1, 3)
ORDER = (2, 1, 3, 0, 4)
F32 = jnp.float32
BF16 = jnp.bfloat16


def rdma(src, dst, send_sem, recv_sem, device):
    return pltpu.make_async_remote_copy(
        src_ref=src,
        dst_ref=dst,
        send_sem=send_sem,
        recv_sem=recv_sem,
        device_id=device,
        device_id_type=MESH,
    )


def greet(devices):
    barrier = pltpu.get_barrier_semaphore()
    for device in devices:
        pl.semaphore_signal(barrier, inc=1, device_id=device, device_id_type=MESH)
    pl.semaphore_wait(barrier, len(devices))


def split2(value):
    high = value.astype(BF16).astype(F32)
    return high, value - high


def exchange(gathered, send, recv, t, e, nt, ne, mid=None):
    right, left, opposite = lax.rem(e + 2, ne), lax.rem(e + ne - 2, ne), lax.rem(e + 4, ne)
    partner = e + 1 - 2 * lax.rem(e, 2)
    slots = [
        e,
        left,
        right,
        opposite,
        partner,
        lax.rem(partner + ne - 2, ne),
        lax.rem(partner + 2, ne),
        lax.rem(partner + 4, ne),
    ]
    started = []

    def go(k, rel, target_k, target_rel, device):
        copy = rdma(
            gathered.at[k, slots[rel]],
            gathered.at[target_k, slots[rel]],
            send.at[len(started)],
            recv.at[target_k, target_rel],
            device,
        )
        copy.start()
        started.append(copy)

    def arrive(k, rel):
        rdma(
            gathered.at[k, slots[rel]],
            gathered.at[k, slots[rel]],
            send.at[0],
            recv.at[k, rel],
            (t, partner),
        ).wait_recv()

    for offset in (1, -1, 2, -2):
        go(REACH, 0, REACH - offset, 0, (lax.rem(t + nt + offset, nt), e))
    if mid is not None:
        mid()
    for k in ORDER:
        if k != REACH:
            arrive(k, 0)
        go(k, 0, k, 1, (t, right))
        go(k, 0, k, 2, (t, left))
        go(k, 0, k, 4, (t, partner))
    for k in ORDER:
        arrive(k, 1)
        if k in FORWARD_RIGHT:
            go(k, 1, k, 3, (t, right))
        go(k, 1, k, 5, (t, partner))
        arrive(k, 2)
        if k not in FORWARD_RIGHT:
            go(k, 2, k, 3, (t, left))
        go(k, 2, k, 6, (t, partner))
    for k in ORDER:
        arrive(k, 3)
        go(k, 3, k, 7, (t, partner))
    for k in ORDER:
        for rel in (4, 5, 6, 7):
            arrive(k, rel)
    for copy in started:
        copy.wait_send()


EXCHANGE_SENDS = 4 + 3 * WINDOW + 3 * WINDOW + WINDOW


def tile_peers(t, e, nt):
    return [(lax.rem(t + nt + offset, nt), e) for offset in (1, -1, 2, -2)]


def ens_peers(t, e, ne):
    return [(t, lax.rem(e + d, ne)) for d in range(1, ne)]


def forecast_kernel(
    nt, ne,
    x, u, loc, cnt, val, err,
    gathered, cols, second, meta,
    hs, hr, tmp, ub, bg, parts, sb, rb,
    halo_s, halo_r, meta_s, meta_r, bulk_s, bulk_r, small_s, small_r, ex_s, ex_r, own_sem,
):
    t, e = lax.axis_index("tile"), lax.axis_index("ens")
    per, levels, rows, width = x.shape
    lr = levels * rows
    col_count = width // ne
    slots = loc.shape[2]

    def fill(m, carry):
        for l in range(levels):
            hs[0, m, l : l + 1, :] = x[m, l, 0:1, :]
            hs[1, m, l : l + 1, :] = x[m, l, rows - 1 : rows, :]
        return carry

    lax.fori_loop(0, per, fill, 0)
    slot_index = lax.broadcasted_iota(jnp.int32, (1, slots), 1)
    for b in range(BATCHES):
        for i in range(3):
            meta[REACH, b, i : i + 1, :] = loc[i, b : b + 1, :].astype(F32)
        meta[REACH, b, 3:4, :] = val[b : b + 1, :]
        meta[REACH, b, 4:5, :] = err[b : b + 1, :]
        meta[REACH, b, 5:6, :] = (slot_index < cnt[b : b + 1, 0:1]).astype(F32)
        meta[REACH, b, 6:8, :] = jnp.zeros((2, slots), F32)
    greet(tile_peers(t, e, nt) + ens_peers(t, e, ne))
    up_tile, down_tile = lax.rem(t + nt - 1, nt), lax.rem(t + 1, nt)
    halos = [
        rdma(hs.at[1], hr.at[0], halo_s.at[0], halo_r.at[0], (down_tile, e)),
        rdma(hs.at[0], hr.at[1], halo_s.at[1], halo_r.at[1], (up_tile, e)),
    ]
    for copy in halos:
        copy.start()
    metas = []
    for i, offset in enumerate((1, -1, 2, -2)):
        copy = rdma(
            meta.at[REACH],
            meta.at[REACH - offset],
            meta_s.at[i],
            meta_r.at[i],
            (lax.rem(t + nt + offset, nt), e),
        )
        copy.start()
        metas.append(copy)
    for a in range(2):
        for l in range(levels):
            ub[a, l * rows : (l + 1) * rows, :] = u[a, l]
    for copy in halos:
        copy.wait_recv()
    has_up = jnp.where(t > 0, 1.0, 0.0).astype(F32)
    has_down = jnp.where(t < nt - 1, 1.0, 0.0).astype(F32)

    def step(m, carry):
        for l in range(levels):
            tmp[l * rows : (l + 1) * rows, :] = x[m, l]
        c = tmp[...]
        above = hr[0, m] * has_up
        below = hr[1, m] * has_down
        row = lax.broadcasted_iota(jnp.int32, (lr, width), 0)
        col = lax.broadcasted_iota(jnp.int32, (lr, width), 1)
        up = pltpu.roll(c, 1, 0)
        down = pltpu.roll(c, lr - 1, 0)
        for l in range(levels):
            up = jnp.where(row == l * rows, above[l : l + 1], up)
            down = jnp.where(row == l * rows + rows - 1, below[l : l + 1], down)
        west = jnp.where(col == 0, 0.0, pltpu.roll(c, 1, 1))
        east = jnp.where(col == width - 1, 0.0, pltpu.roll(c, width - 1, 1))
        wr, wc = ub[0], ub[1]
        tendency = (
            jnp.maximum(wr, 0.0) * (c - up)
            + jnp.minimum(wr, 0.0) * (down - c)
            + jnp.maximum(wc, 0.0) * (c - west)
            + jnp.minimum(wc, 0.0) * (east - c)
        )
        ahead = c - tendency + SPREAD_RATE * (up + down + west + east - 4.0 * c)
        for i in range(width // LANES):
            bg[i, m] = ahead[:, i * LANES : (i + 1) * LANES]
        return carry

    lax.fori_loop(0, per, step, 0)

    pieces = col_count // LANES

    def block_of(device):
        return pl.ds(device * pieces, pieces)

    bulks = []

    def send_bulk(d):
        peer = lax.rem(e + d, ne)
        copy = rdma(
            bg.at[block_of(peer)],
            cols.at[:, pl.ds(e * per, per)],
            bulk_s.at[d],
            bulk_r.at[d],
            (t, peer),
        )
        copy.start()
        bulks.append(copy)

    own = pltpu.make_async_copy(bg.at[block_of(e)], cols.at[:, pl.ds(e * per, per)], own_sem)
    own.start()
    for d in (1, 2, ne - 1, ne - 2):
        send_bulk(d)

    def split(kk, carry):
        f = jnp.concatenate(
            [bg[2 * kk].reshape(per * lr, LANES), bg[2 * kk + 1].reshape(per * lr, LANES)], axis=1
        )
        high, rest = split2(f)
        middle, low = split2(rest)
        parts[kk] = jnp.concatenate([high, middle, low], axis=0).astype(BF16)
        return carry

    lax.fori_loop(0, width // BLOCK, split, 0)
    held = per * lr
    for b in range(BATCHES):

        def pick(j, carry):
            here = pl.ds(pl.multiple_of(j * BLOCK, BLOCK), BLOCK)
            place = loc[2, b : b + 1, here] * rows + (loc[0, b : b + 1, here] - t * rows)
            column = loc[1, b : b + 1, here]
            down = lax.broadcasted_iota(jnp.int32, (BLOCK, BLOCK), 0)
            total = jnp.zeros((3 * held, BLOCK), F32)
            for kk in range(width // BLOCK):
                hot = jnp.where(down == column - kk * BLOCK, 1.0, 0.0).astype(BF16)
                total += jnp.dot(parts[kk], hot, preferred_element_type=F32)
            value = total[0:held] + total[held : 2 * held] + total[2 * held :]
            mine = lax.broadcasted_iota(jnp.int32, (lr, BLOCK), 0) == place
            value = jnp.where(mine[None], value.reshape(per, lr, BLOCK), 0.0)
            value = jnp.sum(value, axis=1)
            for half in range(BLOCK // LANES):
                sb[j * (BLOCK // LANES) + half, b, 0:per, :] = value[
                    :, half * LANES : (half + 1) * LANES
                ]
            return carry

        lax.fori_loop(0, slots // BLOCK, pick, 0)

    smalls = []
    for d in (4, 3, 5, 2, 6, 1, 7):
        peer = lax.rem(e + d, ne)
        copy = rdma(sb.at[peer], rb.at[e], small_s.at[d], small_r.at[d], (t, peer))
        copy.start()
        smalls.append(copy)
    for d in (4, 3, 5):
        send_bulk(d)
    rb[e] = sb[e]
    for d in range(1, ne):
        source = lax.rem(e + ne - d, ne)
        rdma(
            sb.at[source], rb.at[source], small_s.at[d], small_r.at[d], (t, source)
        ).wait_recv()
    for s in range(ne):
        gathered[REACH, e, s * per : (s + 1) * per, :] = rb[s, 0, 0:per, :]
        second[s * per : (s + 1) * per, :] = rb[s, 1, 0:per, :]
    exchange(gathered, ex_s, ex_r, t, e, nt, ne)
    own.wait()
    for d in range(1, ne):
        source = lax.rem(e + ne - d, ne)
        rdma(
            bg.at[block_of(source)],
            cols.at[:, pl.ds(source * per, per)],
            bulk_s.at[d],
            bulk_r.at[d],
            (t, source),
        ).wait_recv()
    for i, offset in enumerate((1, -1, 2, -2)):
        rdma(
            meta.at[REACH],
            meta.at[REACH - offset],
            meta_s.at[i],
            meta_r.at[i],
            (up_tile, e),
        ).wait_recv()
    for copy in halos + metas + bulks + smalls:
        copy.wait_send()


def gather_kernel(nt, ne, prior, gathered, ex_s, ex_r):
    t, e = lax.axis_index("tile"), lax.axis_index("ens")
    gathered[REACH, e] = prior[...]
    partner = e + 1 - 2 * lax.rem(e, 2)
    ring = [(t, lax.rem(e + 2, ne)), (t, lax.rem(e + ne - 2, ne)), (t, partner)]
    greet(tile_peers(t, e, nt) + ring)
    exchange(gathered, ex_s, ex_r, t, e, nt, ne)


def spread_kernel(nt, ne, cols, out, grid, send, recv):
    t, e = lax.axis_index("tile"), lax.axis_index("ens")
    per, levels, rows, width = out.shape
    pieces = width // ne // LANES
    greet(ens_peers(t, e, ne))

    def block_of(device):
        return pl.ds(device * pieces, pieces)

    copies = []
    for d in (4, 3, 5, 2, 6, 1, 7):
        peer = lax.rem(e + d, ne)
        copy = rdma(
            cols.at[:, pl.ds(peer * per, per)],
            grid.at[block_of(e)],
            send.at[d],
            recv.at[d],
            (t, peer),
        )
        copy.start()
        copies.append(copy)
    own = pltpu.make_async_copy(
        cols.at[:, pl.ds(e * per, per)], grid.at[block_of(e)], send.at[0]
    )
    own.start()
    own.wait()
    for d in range(1, ne):
        source = lax.rem(e + ne - d, ne)
        rdma(
            cols.at[:, pl.ds(source * per, per)],
            grid.at[block_of(source)],
            send.at[d],
            recv.at[d],
            (t, source),
        ).wait_recv()

    def put(m, carry):
        for l in range(levels):
            for i in range(width // LANES):
                out[m, l, :, i * LANES : (i + 1) * LANES] = grid[i, m, l * rows : (l + 1) * rows, :]
        return carry

    lax.fori_loop(0, per, put, 0)
    for copy in copies:
        copy.wait_send()


def update_kernel(nt, ne, batch, look_ahead, *refs):
    if look_ahead:
        gathered, meta, cols, second, out, prior, weights, shifts, states, total, ahead = refs
    else:
        gathered, meta, cols, out, weights, shifts, states, total = refs
    t, e = lax.axis_index("tile"), lax.axis_index("ens")
    members = gathered.shape[2]
    slices = gathered.shape[1]
    halves = cols.shape[0]
    lr = cols.shape[1] // members
    levels = 2
    rows = lr // levels
    width = halves * LANES
    col_total = width * ne
    inverse_col = 1.0 / float(col_total // 2)
    inverse_row = 1.0 / float(REACH * rows)

    def blocks(k):
        live = jnp.sum(meta[k, batch, 5:6, :])
        return (live.astype(jnp.int32) + (BLOCK - 1)) // BLOCK

    def prepare(k, carry):
        def piece(s, inner):
            here = pl.ds(pl.multiple_of(s * LANES, LANES), LANES)
            p = gathered[k, s]
            lev = meta[k, batch, 2:3, here]
            value = meta[k, batch, 3:4, here]
            error = meta[k, batch, 4:5, here]
            live = meta[k, batch, 5:6, here]
            average = jnp.sum(p, axis=0, keepdims=True) / members
            deviation = p - average
            variance = (
                jnp.sum(deviation * deviation, axis=0, keepdims=True) / (members - 1) + EPSILON
            )
            combined = variance + error
            shrink = jnp.sqrt(error / combined)
            mean_post = (error * average + variance * value) / combined
            shift = live * ((shrink - 1.0) * deviation + (mean_post - average))
            weight = deviation * (live / ((members - 1) * variance))
            high, low = split2(weight)
            for l in range(levels):
                factor = jnp.where(lev == float(l), 1.0, 0.5)
                scaled = (high * factor).astype(BF16)
                weights[k, l, 0:members, here] = scaled
                weights[k, l, members : 2 * members, here] = scaled
                weights[k, l, 2 * members : 3 * members, here] = (low * factor).astype(BF16)
            both = jnp.concatenate(split2(shift), axis=0)
            shifts[k, here, :] = both.T.astype(BF16)
            return inner

        lax.fori_loop(0, blocks(k) * (BLOCK // LANES), piece, 0)
        return carry

    lax.fori_loop(0, WINDOW, prepare, 0)

    def cell_major(value):
        high, low = split2(value)
        return jnp.concatenate([high, low, high], axis=0).T.astype(BF16)

    def member_major(value):
        turned = value.T
        return turned[0:members] + turned[members : 2 * members]

    for i in range(lr):
        here = pl.ds(i, members, stride=lr)
        states[i] = cell_major(jnp.concatenate([cols[h, here, :] for h in range(halves)], axis=1))
    total[...] = jnp.zeros_like(total)

    def apply(gain, k, here):
        high = gain.astype(BF16)
        low = (gain - high.astype(F32)).astype(BF16)
        right = shifts[k, here, :]
        return jnp.dot(high, right, preferred_element_type=F32) + jnp.dot(
            low, right, preferred_element_type=F32
        )

    if look_ahead:
        mine = pl.ds(pl.multiple_of(e * LANES, LANES), LANES)
        places = meta[REACH, batch + 1, :, mine].T
        cell_row, cell_col, cell_lev = places[:, 0:1], places[:, 1:2], places[:, 2:3]
        x2 = cell_major(second[...])
        ahead[...] = jnp.zeros_like(ahead)

        def look(k, carry):
            def block(j, inner):
                here = pl.ds(pl.multiple_of(j * BLOCK, BLOCK), BLOCK)
                row_gap = (cell_row - meta[k, batch, 0:1, here]) * inverse_row
                col_gap = (cell_col - meta[k, batch, 1:2, here]) * inverse_col
                close = jnp.maximum(1.0 - row_gap * row_gap - col_gap * col_gap, 0.0)
                first = jnp.dot(x2, weights[k, 0, :, here], preferred_element_type=F32)
                other = jnp.dot(x2, weights[k, 1, :, here], preferred_element_type=F32)
                gain = jnp.where(cell_lev == 0.0, first, other) * (close * close)
                ahead[...] += apply(gain, k, here)
                return inner

            lax.fori_loop(0, blocks(k), block, 0)
            return carry

        lax.fori_loop(0, WINDOW, look, 0)
        prior[...] = second[...] + member_major(ahead[...])

    cell_col = (lax.broadcasted_iota(jnp.int32, (width, BLOCK), 0) + e * width).astype(
        F32
    ) * inverse_col
    first_row = (t * rows).astype(F32)

    def main(k, carry):
        def block(j, inner):
            here = pl.ds(pl.multiple_of(j * BLOCK, BLOCK), BLOCK)
            col_gap = cell_col - meta[k, batch, 1:2, here] * inverse_col
            col_part = col_gap * col_gap
            obs_row = meta[k, batch, 0:1, here]
            for r in range(rows):
                row_gap = (first_row + float(r) - obs_row) * inverse_row
                close = jnp.maximum((1.0 - row_gap * row_gap) - col_part, 0.0)
                close = close * close
                for l in range(levels):
                    i = l * rows + r
                    covariance = jnp.dot(
                        states[i], weights[k, l, :, here], preferred_element_type=F32
                    )
                    total[i] += apply(covariance * close, k, here)
            return inner

        lax.fori_loop(0, blocks(k), block, 0)
        return carry

    lax.fori_loop(0, WINDOW, main, 0)
    for i in range(lr):
        here = pl.ds(i, members, stride=lr)
        change = member_major(total[i])
        for h in range(halves):
            out[h, here, :] = cols[h, here, :] + change[:, h * LANES : (h + 1) * LANES]


def on_device(nt, ne, x, u, loc, cnt, val, err):
    per, levels, rows, width = x.shape
    lr = levels * rows
    members = per * ne
    slots = val.shape[1]
    col_count = width // ne
    vmem = pl.BlockSpec(memory_space=VMEM)
    dma = pltpu.SemaphoreType.DMA
    window = jax.ShapeDtypeStruct((WINDOW, ne, members, LANES), F32)
    pieces = col_count // LANES
    flat = jax.ShapeDtypeStruct((pieces, members * lr, LANES), F32)
    gathered, cols, second, meta = pl.pallas_call(
        functools.partial(forecast_kernel, nt, ne),
        out_shape=[
            window,
            jax.ShapeDtypeStruct((pieces, members, lr, LANES), F32),
            jax.ShapeDtypeStruct((members, LANES), F32),
            jax.ShapeDtypeStruct((WINDOW, BATCHES, 8, slots), F32),
        ],
        in_specs=[vmem] * 6,
        out_specs=[vmem] * 4,
        scratch_shapes=[
            VMEM((2, per, levels, width), F32),
            VMEM((2, per, levels, width), F32),
            VMEM((lr, width), F32),
            VMEM((2, lr, width), F32),
            VMEM((width // LANES, per, lr, LANES), F32),
            VMEM((width // BLOCK, 3 * per * lr, BLOCK), BF16),
            VMEM((ne, BATCHES, 16, LANES), F32),
            VMEM((ne, BATCHES, 16, LANES), F32),
            dma((2,)),
            dma((2,)),
            dma((4,)),
            dma((4,)),
            dma((ne,)),
            dma((ne,)),
            dma((ne,)),
            dma((ne,)),
            dma((EXCHANGE_SENDS,)),
            dma((WINDOW, ne)),
            dma,
        ],
        compiler_params=pltpu.CompilerParams(collective_id=0, has_side_effects=True),
        name="forecast",
    )(x, u, loc, cnt, val, err)
    cols = cols.reshape(flat.shape)
    work = [
        VMEM((WINDOW, levels, 3 * members, slots), BF16),
        VMEM((WINDOW, slots, 2 * members), BF16),
        VMEM((lr, col_count, 3 * members), BF16),
        VMEM((lr, col_count, 2 * members), F32),
    ]
    cols, prior = pl.pallas_call(
        functools.partial(update_kernel, nt, ne, 0, True),
        out_shape=[flat, jax.ShapeDtypeStruct((members, LANES), F32)],
        in_specs=[vmem] * 4,
        out_specs=[vmem] * 2,
        scratch_shapes=work + [VMEM((LANES, 2 * members), F32)],
        name="first_update",
    )(gathered, meta, cols, second)
    gathered = pl.pallas_call(
        functools.partial(gather_kernel, nt, ne),
        out_shape=window,
        in_specs=[vmem],
        out_specs=vmem,
        scratch_shapes=[dma((EXCHANGE_SENDS,)), dma((WINDOW, ne))],
        compiler_params=pltpu.CompilerParams(collective_id=1, has_side_effects=True),
        name="gather",
    )(prior)
    cols = pl.pallas_call(
        functools.partial(update_kernel, nt, ne, 1, False),
        out_shape=flat,
        in_specs=[vmem] * 3,
        out_specs=vmem,
        scratch_shapes=work,
        name="second_update",
    )(gathered, meta, cols)
    return pl.pallas_call(
        functools.partial(spread_kernel, nt, ne),
        out_shape=jax.ShapeDtypeStruct(x.shape, F32),
        in_specs=[vmem],
        out_specs=vmem,
        scratch_shapes=[VMEM((width // LANES, per, lr, LANES), F32), dma((ne,)), dma((ne,))],
        compiler_params=pltpu.CompilerParams(collective_id=2, has_side_effects=True),
        name="spread",
    )(cols.reshape(pieces, members, lr, LANES))


def solution(mesh):
    in_specs = (
        P("ens", None, "tile", None),
        P(None, None, "tile", None),
        P(None, None, "tile"),
        P(None, "tile"),
        P(None, "tile"),
        P(None, "tile"),
    )
    out_specs = P("ens", None, "tile", None)
    body = functools.partial(on_device, mesh.shape["tile"], mesh.shape["ens"])
    return jax.shard_map(body, mesh=mesh, in_specs=in_specs, out_specs=out_specs, check_vma=False)
```

```python
import functools

import jax
import jax.numpy as jnp
from jax import lax
from jax.experimental import pallas as pl
from jax.experimental.pallas import tpu as pltpu
from jax.sharding import PartitionSpec as P

BATCHES = 2
REACH = 2
WINDOW = 2 * REACH + 1
SPREAD_RATE = 0.05
EPSILON = 1e-06
MESH = pl.DeviceIdType.MESH
VMEM = pltpu.VMEM
LANES = 128
BLOCK = 256
FORWARD_RIGHT = (2, 1, 3)
ORDER = (2, 1, 3, 0, 4)
F32 = jnp.float32
BF16 = jnp.bfloat16


def rdma(src, dst, send_sem, recv_sem, device):
    return pltpu.make_async_remote_copy(
        src_ref=src,
        dst_ref=dst,
        send_sem=send_sem,
        recv_sem=recv_sem,
        device_id=device,
        device_id_type=MESH,
    )


def greet(devices):
    barrier = pltpu.get_barrier_semaphore()
    for device in devices:
        pl.semaphore_signal(barrier, inc=1, device_id=device, device_id_type=MESH)
    pl.semaphore_wait(barrier, len(devices))


def split2(value):
    high = value.astype(BF16).astype(F32)
    return high, value - high


def exchange(gathered, send, recv, t, e, nt, ne, mid=None):
    right, left, opposite = lax.rem(e + 2, ne), lax.rem(e + ne - 2, ne), lax.rem(e + 4, ne)
    partner = e + 1 - 2 * lax.rem(e, 2)
    slots = [
        e,
        left,
        right,
        opposite,
        partner,
        lax.rem(partner + ne - 2, ne),
        lax.rem(partner + 2, ne),
        lax.rem(partner + 4, ne),
    ]
    started = []

    def go(k, rel, target_k, target_rel, device):
        copy = rdma(
            gathered.at[k, slots[rel]],
            gathered.at[target_k, slots[rel]],
            send.at[len(started)],
            recv.at[target_k, target_rel],
            device,
        )
        copy.start()
        started.append(copy)

    def arrive(k, rel):
        rdma(
            gathered.at[k, slots[rel]],
            gathered.at[k, slots[rel]],
            send.at[0],
            recv.at[k, rel],
            (t, partner),
        ).wait_recv()

    for offset in (1, -1, 2, -2):
        go(REACH, 0, REACH - offset, 0, (lax.rem(t + nt + offset, nt), e))
    if mid is not None:
        mid()
    for k in ORDER:
        if k != REACH:
            arrive(k, 0)
        go(k, 0, k, 1, (t, right))
        go(k, 0, k, 2, (t, left))
        go(k, 0, k, 4, (t, partner))
    for k in ORDER:
        arrive(k, 1)
        if k in FORWARD_RIGHT:
            go(k, 1, k, 3, (t, right))
        go(k, 1, k, 5, (t, partner))
        arrive(k, 2)
        if k not in FORWARD_RIGHT:
            go(k, 2, k, 3, (t, left))
        go(k, 2, k, 6, (t, partner))
    for k in ORDER:
        arrive(k, 3)
        go(k, 3, k, 7, (t, partner))
    for k in ORDER:
        for rel in (4, 5, 6, 7):
            arrive(k, rel)
    for copy in started:
        copy.wait_send()


EXCHANGE_SENDS = 4 + 3 * WINDOW + 3 * WINDOW + WINDOW


def tile_peers(t, e, nt):
    return [(lax.rem(t + nt + offset, nt), e) for offset in (1, -1, 2, -2)]


def ens_peers(t, e, ne):
    return [(t, lax.rem(e + d, ne)) for d in range(1, ne)]


def forecast_kernel(
    nt, ne,
    x, u, loc, cnt, val, err,
    gathered, cols, second, meta,
    hs, hr, tmp, ub, bg, parts, sb, rb,
    halo_s, halo_r, meta_s, meta_r, bulk_s, bulk_r, small_s, small_r, ex_s, ex_r, own_sem,
):
    t, e = lax.axis_index("tile"), lax.axis_index("ens")
    per, levels, rows, width = x.shape
    lr = levels * rows
    col_count = width // ne
    slots = loc.shape[2]

    def fill(m, carry):
        for l in range(levels):
            hs[0, m, l : l + 1, :] = x[m, l, 0:1, :]
            hs[1, m, l : l + 1, :] = x[m, l, rows - 1 : rows, :]
        return carry

    lax.fori_loop(0, per, fill, 0)
    slot_index = lax.broadcasted_iota(jnp.int32, (1, slots), 1)
    for b in range(BATCHES):
        for i in range(3):
            meta[REACH, b, i : i + 1, :] = loc[i, b : b + 1, :].astype(F32)
        meta[REACH, b, 3:4, :] = val[b : b + 1, :]
        meta[REACH, b, 4:5, :] = err[b : b + 1, :]
        meta[REACH, b, 5:6, :] = (slot_index < cnt[0:1, b : b + 1]).astype(F32)
        meta[REACH, b, 6:8, :] = jnp.zeros((2, slots), F32)
    greet(tile_peers(t, e, nt) + ens_peers(t, e, ne))
    up_tile, down_tile = lax.rem(t + nt - 1, nt), lax.rem(t + 1, nt)
    halos = [
        rdma(hs.at[1], hr.at[0], halo_s.at[0], halo_r.at[0], (down_tile, e)),
        rdma(hs.at[0], hr.at[1], halo_s.at[1], halo_r.at[1], (up_tile, e)),
    ]
    for copy in halos:
        copy.start()
    metas = []
    for i, offset in enumerate((1, -1, 2, -2)):
        copy = rdma(
            meta.at[REACH],
            meta.at[REACH - offset],
            meta_s.at[i],
            meta_r.at[i],
            (lax.rem(t + nt + offset, nt), e),
        )
        copy.start()
        metas.append(copy)
    for a in range(2):
        for l in range(levels):
            ub[a, l * rows : (l + 1) * rows, :] = u[a, l]
    for copy in halos:
        copy.wait_recv()
    has_up = jnp.where(t > 0, 1.0, 0.0).astype(F32)
    has_down = jnp.where(t < nt - 1, 1.0, 0.0).astype(F32)

    def step(m, carry):
        for l in range(levels):
            tmp[l * rows : (l + 1) * rows, :] = x[m, l]
        c = tmp[...]
        above = hr[0, m] * has_up
        below = hr[1, m] * has_down
        row = lax.broadcasted_iota(jnp.int32, (lr, width), 0)
        col = lax.broadcasted_iota(jnp.int32, (lr, width), 1)
        up = pltpu.roll(c, 1, 0)
        down = pltpu.roll(c, lr - 1, 0)
        for l in range(levels):
            up = jnp.where(row == l * rows, above[l : l + 1], up)
            down = jnp.where(row == l * rows + rows - 1, below[l : l + 1], down)
        west = jnp.where(col == 0, 0.0, pltpu.roll(c, 1, 1))
        east = jnp.where(col == width - 1, 0.0, pltpu.roll(c, width - 1, 1))
        wr, wc = ub[0], ub[1]
        tendency = (
            jnp.maximum(wr, 0.0) * (c - up)
            + jnp.minimum(wr, 0.0) * (down - c)
            + jnp.maximum(wc, 0.0) * (c - west)
            + jnp.minimum(wc, 0.0) * (east - c)
        )
        ahead = c - tendency + SPREAD_RATE * (up + down + west + east - 4.0 * c)
        for i in range(width // LANES):
            bg[i, m] = ahead[:, i * LANES : (i + 1) * LANES]
        return carry

    lax.fori_loop(0, per, step, 0)

    pieces = col_count // LANES

    def block_of(device):
        return pl.ds(device * pieces, pieces)

    bulks = []

    def send_bulk(d):
        peer = lax.rem(e + d, ne)
        copy = rdma(
            bg.at[block_of(peer)],
            cols.at[:, pl.ds(e * per, per)],
            bulk_s.at[d],
            bulk_r.at[d],
            (t, peer),
        )
        copy.start()
        bulks.append(copy)

    own = pltpu.make_async_copy(bg.at[block_of(e)], cols.at[:, pl.ds(e * per, per)], own_sem)
    own.start()
    for d in (1, 2, ne - 1, ne - 2):
        send_bulk(d)

    def split(kk, carry):
        f = jnp.concatenate(
            [bg[2 * kk].reshape(per * lr, LANES), bg[2 * kk + 1].reshape(per * lr, LANES)], axis=1
        )
        high, rest = split2(f)
        middle, low = split2(rest)
        parts[kk] = jnp.concatenate([high, middle, low], axis=0).astype(BF16)
        return carry

    lax.fori_loop(0, width // BLOCK, split, 0)
    held = per * lr
    for b in range(BATCHES):

        def pick(j, carry):
            here = pl.ds(pl.multiple_of(j * BLOCK, BLOCK), BLOCK)
            place = loc[2, b : b + 1, here] * rows + (loc[0, b : b + 1, here] - t * rows)
            column = loc[1, b : b + 1, here]
            down = lax.broadcasted_iota(jnp.int32, (BLOCK, BLOCK), 0)
            total = jnp.zeros((3 * held, BLOCK), F32)
            for kk in range(width // BLOCK):
                hot = jnp.where(down == column - kk * BLOCK, 1.0, 0.0).astype(BF16)
                total += jnp.dot(parts[kk], hot, preferred_element_type=F32)
            value = total[0:held] + total[held : 2 * held] + total[2 * held :]
            mine = lax.broadcasted_iota(jnp.int32, (lr, BLOCK), 0) == place
            value = jnp.where(mine[None], value.reshape(per, lr, BLOCK), 0.0)
            value = jnp.sum(value, axis=1)
            for half in range(BLOCK // LANES):
                sb[j * (BLOCK // LANES) + half, b, 0:per, :] = value[
                    :, half * LANES : (half + 1) * LANES
                ]
            return carry

        lax.fori_loop(0, slots // BLOCK, pick, 0)

    smalls = []
    for d in (4, 3, 5, 2, 6, 1, 7):
        peer = lax.rem(e + d, ne)
        copy = rdma(sb.at[peer], rb.at[e], small_s.at[d], small_r.at[d], (t, peer))
        copy.start()
        smalls.append(copy)
    for d in (4, 3, 5):
        send_bulk(d)
    rb[e] = sb[e]
    for d in range(1, ne):
        source = lax.rem(e + ne - d, ne)
        rdma(
            sb.at[source], rb.at[source], small_s.at[d], small_r.at[d], (t, source)
        ).wait_recv()
    for s in range(ne):
        gathered[REACH, e, s * per : (s + 1) * per, :] = rb[s, 0, 0:per, :]
        second[s * per : (s + 1) * per, :] = rb[s, 1, 0:per, :]
    exchange(gathered, ex_s, ex_r, t, e, nt, ne)
    own.wait()
    for d in range(1, ne):
        source = lax.rem(e + ne - d, ne)
        rdma(
            bg.at[block_of(source)],
            cols.at[:, pl.ds(source * per, per)],
            bulk_s.at[d],
            bulk_r.at[d],
            (t, source),
        ).wait_recv()
    for i, offset in enumerate((1, -1, 2, -2)):
        rdma(
            meta.at[REACH],
            meta.at[REACH - offset],
            meta_s.at[i],
            meta_r.at[i],
            (up_tile, e),
        ).wait_recv()
    for copy in halos + metas + bulks + smalls:
        copy.wait_send()


def gather_kernel(nt, ne, prior, gathered, ex_s, ex_r):
    t, e = lax.axis_index("tile"), lax.axis_index("ens")
    gathered[REACH, e] = prior[...]
    partner = e + 1 - 2 * lax.rem(e, 2)
    ring = [(t, lax.rem(e + 2, ne)), (t, lax.rem(e + ne - 2, ne)), (t, partner)]
    greet(tile_peers(t, e, nt) + ring)
    exchange(gathered, ex_s, ex_r, t, e, nt, ne)


def spread_kernel(nt, ne, cols, out, grid, send, recv):
    t, e = lax.axis_index("tile"), lax.axis_index("ens")
    per, levels, rows, width = out.shape
    pieces = width // ne // LANES
    greet(ens_peers(t, e, ne))

    def block_of(device):
        return pl.ds(device * pieces, pieces)

    copies = []
    for d in (4, 3, 5, 2, 6, 1, 7):
        peer = lax.rem(e + d, ne)
        copy = rdma(
            cols.at[:, pl.ds(peer * per, per)],
            grid.at[block_of(e)],
            send.at[d],
            recv.at[d],
            (t, peer),
        )
        copy.start()
        copies.append(copy)
    own = pltpu.make_async_copy(
        cols.at[:, pl.ds(e * per, per)], grid.at[block_of(e)], send.at[0]
    )
    own.start()
    own.wait()
    for d in range(1, ne):
        source = lax.rem(e + ne - d, ne)
        rdma(
            cols.at[:, pl.ds(source * per, per)],
            grid.at[block_of(source)],
            send.at[d],
            recv.at[d],
            (t, source),
        ).wait_recv()

    def put(m, carry):
        for l in range(levels):
            for i in range(width // LANES):
                out[m, l, :, i * LANES : (i + 1) * LANES] = grid[i, m, l * rows : (l + 1) * rows, :]
        return carry

    lax.fori_loop(0, per, put, 0)
    for copy in copies:
        copy.wait_send()


def update_kernel(nt, ne, batch, look_ahead, *refs):
    if look_ahead:
        gathered, meta, cols, second, out, prior, weights, shifts, states, total, closes, gains, ahead = refs
    else:
        gathered, meta, cols, out, weights, shifts, states, total, closes, gains = refs
    t, e = lax.axis_index("tile"), lax.axis_index("ens")
    members = gathered.shape[2]
    slices = gathered.shape[1]
    halves = cols.shape[0]
    lr = cols.shape[1] // members
    levels = 2
    rows = lr // levels
    width = halves * LANES
    span = rows * width
    col_total = width * ne
    inverse_col = 1.0 / float(col_total // 2)
    inverse_row = 1.0 / float(REACH * rows)

    def blocks(k):
        live = jnp.sum(meta[k, batch, 5:6, :])
        return (live.astype(jnp.int32) + (BLOCK - 1)) // BLOCK

    def prepare(k, carry):
        def piece(s, inner):
            here = pl.ds(pl.multiple_of(s * BLOCK, BLOCK), BLOCK)
            p = jnp.concatenate([gathered[k, 2 * s], gathered[k, 2 * s + 1]], axis=1)
            lev = meta[k, batch, 2:3, here]
            value = meta[k, batch, 3:4, here]
            error = meta[k, batch, 4:5, here]
            live = meta[k, batch, 5:6, here]
            average = jnp.sum(p, axis=0, keepdims=True) / members
            deviation = p - average
            variance = (
                jnp.sum(deviation * deviation, axis=0, keepdims=True) / (members - 1) + EPSILON
            )
            combined = variance + error
            shrink = jnp.sqrt(error / combined)
            mean_post = (error * average + variance * value) / combined
            shift = live * ((shrink - 1.0) * deviation + (mean_post - average))
            weight = deviation * (live / ((members - 1) * variance))
            high, low = split2(weight)
            for l in range(levels):
                factor = jnp.where(lev == float(l), 1.0, 0.5)
                scaled = (high * factor).astype(BF16)
                weights[k, l, 0:members, here] = scaled
                weights[k, l, members : 2 * members, here] = scaled
                weights[k, l, 2 * members : 3 * members, here] = (low * factor).astype(BF16)
            both = jnp.concatenate(split2(shift), axis=0)
            shifts[k, here, :] = both.T.astype(BF16)
            return inner

        lax.fori_loop(0, blocks(k), piece, 0)
        return carry

    lax.fori_loop(0, WINDOW, prepare, 0)

    def cell_major(value):
        high, low = split2(value)
        return jnp.concatenate([high, low, high], axis=0).T.astype(BF16)

    def member_major(value):
        turned = value.T
        return turned[0:members] + turned[members : 2 * members]

    for i in range(lr):
        here = pl.ds(i, members, stride=lr)
        states[i // rows, i % rows * width : (i % rows + 1) * width, :] = cell_major(jnp.concatenate([cols[h, here, :] for h in range(halves)], axis=1))
    total[...] = jnp.zeros_like(total)

    def apply(gain, k, here):
        high = gain.astype(BF16)
        low = (gain - high.astype(F32)).astype(BF16)
        right = shifts[k, here, :]
        return jnp.dot(high, right, preferred_element_type=F32) + jnp.dot(
            low, right, preferred_element_type=F32
        )

    if look_ahead:
        mine = pl.ds(pl.multiple_of(e * LANES, LANES), LANES)
        places = meta[REACH, batch + 1, :, mine].T
        cell_row, cell_col, cell_lev = places[:, 0:1], places[:, 1:2], places[:, 2:3]
        x2 = cell_major(second[...])
        ahead[...] = jnp.zeros_like(ahead)

        def look(k, carry):
            def block(j, inner):
                here = pl.ds(pl.multiple_of(j * BLOCK, BLOCK), BLOCK)
                row_gap = (cell_row - meta[k, batch, 0:1, here]) * inverse_row
                col_gap = (cell_col - meta[k, batch, 1:2, here]) * inverse_col
                close = jnp.maximum(1.0 - row_gap * row_gap - col_gap * col_gap, 0.0)
                first = jnp.dot(x2, weights[k, 0, :, here], preferred_element_type=F32)
                other = jnp.dot(x2, weights[k, 1, :, here], preferred_element_type=F32)
                gain = jnp.where(cell_lev == 0.0, first, other) * (close * close)
                ahead[...] += apply(gain, k, here)
                return inner

            lax.fori_loop(0, blocks(k), block, 0)
            return carry

        lax.fori_loop(0, WINDOW, look, 0)
        prior[...] = second[...] + member_major(ahead[...])

    cell_col = (lax.broadcasted_iota(jnp.int32, (width, BLOCK), 0) + e * width).astype(
        F32
    ) * inverse_col
    first_row = (t * rows).astype(F32)

    def main(k, carry):
        def block(j, inner):
            here = pl.ds(pl.multiple_of(j * BLOCK, BLOCK), BLOCK)
            col_gap = cell_col - meta[k, batch, 1:2, here] * inverse_col
            col_part = col_gap * col_gap
            obs_row = meta[k, batch, 0:1, here]
            for r in range(rows):
                row_gap = (first_row + float(r) - obs_row) * inverse_row
                close = jnp.maximum((1.0 - row_gap * row_gap) - col_part, 0.0)
                closes[r * width : (r + 1) * width, :] = close * close
            for l in range(levels):
                covariance = jnp.dot(states[l], weights[k, l, :, here], preferred_element_type=F32)
                gain = covariance * closes[...]
                high = gain.astype(BF16)
                low = (gain - high.astype(F32)).astype(BF16)
                gains[l * span : (l + 1) * span, :] = jnp.concatenate([high, low], axis=1)
            right = shifts[k, here, :]
            right = jnp.concatenate([right, right], axis=0)
            total[...] += jnp.dot(gains[...], right, preferred_element_type=F32)
            return inner

        lax.fori_loop(0, blocks(k), block, 0)
        return carry

    lax.fori_loop(0, WINDOW, main, 0)
    for i in range(lr):
        here = pl.ds(i, members, stride=lr)
        change = member_major(total[i * width : (i + 1) * width, :])
        for h in range(halves):
            out[h, here, :] = cols[h, here, :] + change[:, h * LANES : (h + 1) * LANES]


def on_device(nt, ne, x, u, loc, cnt, val, err):
    per, levels, rows, width = x.shape
    lr = levels * rows
    members = per * ne
    slots = val.shape[1]
    col_count = width // ne
    vmem = pl.BlockSpec(memory_space=VMEM)
    dma = pltpu.SemaphoreType.DMA
    window = jax.ShapeDtypeStruct((WINDOW, ne, members, LANES), F32)
    pieces = col_count // LANES
    flat = jax.ShapeDtypeStruct((pieces, members * lr, LANES), F32)
    gathered, cols, second, meta = pl.pallas_call(
        functools.partial(forecast_kernel, nt, ne),
        out_shape=[
            window,
            jax.ShapeDtypeStruct((pieces, members, lr, LANES), F32),
            jax.ShapeDtypeStruct((members, LANES), F32),
            jax.ShapeDtypeStruct((WINDOW, BATCHES, 8, slots), F32),
        ],
        in_specs=[vmem] * 6,
        out_specs=[vmem] * 4,
        scratch_shapes=[
            VMEM((2, per, levels, width), F32),
            VMEM((2, per, levels, width), F32),
            VMEM((lr, width), F32),
            VMEM((2, lr, width), F32),
            VMEM((width // LANES, per, lr, LANES), F32),
            VMEM((width // BLOCK, 3 * per * lr, BLOCK), BF16),
            VMEM((ne, BATCHES, 16, LANES), F32),
            VMEM((ne, BATCHES, 16, LANES), F32),
            dma((2,)),
            dma((2,)),
            dma((4,)),
            dma((4,)),
            dma((ne,)),
            dma((ne,)),
            dma((ne,)),
            dma((ne,)),
            dma((EXCHANGE_SENDS,)),
            dma((WINDOW, ne)),
            dma,
        ],
        compiler_params=pltpu.CompilerParams(collective_id=0, has_side_effects=True),
        name="forecast",
    )(x, u, loc, cnt.T, val, err)
    cols = cols.reshape(flat.shape)
    work = [
        VMEM((WINDOW, levels, 3 * members, slots), BF16),
        VMEM((WINDOW, slots, 2 * members), BF16),
        VMEM((levels, rows * col_count, 3 * members), BF16),
        VMEM((lr * col_count, 2 * members), F32),
        VMEM((rows * col_count, BLOCK), F32),
        VMEM((lr * col_count, 2 * BLOCK), BF16),
    ]
    cols, prior = pl.pallas_call(
        functools.partial(update_kernel, nt, ne, 0, True),
        out_shape=[flat, jax.ShapeDtypeStruct((members, LANES), F32)],
        in_specs=[vmem] * 4,
        out_specs=[vmem] * 2,
        scratch_shapes=work + [VMEM((LANES, 2 * members), F32)],
        name="first_update",
    )(gathered, meta, cols, second)
    gathered = pl.pallas_call(
        functools.partial(gather_kernel, nt, ne),
        out_shape=window,
        in_specs=[vmem],
        out_specs=vmem,
        scratch_shapes=[dma((EXCHANGE_SENDS,)), dma((WINDOW, ne))],
        compiler_params=pltpu.CompilerParams(collective_id=1, has_side_effects=True),
        name="gather",
    )(prior)
    cols = pl.pallas_call(
        functools.partial(update_kernel, nt, ne, 1, False),
        out_shape=flat,
        in_specs=[vmem] * 3,
        out_specs=vmem,
        scratch_shapes=work,
        name="second_update",
    )(gathered, meta, cols)
    return pl.pallas_call(
        functools.partial(spread_kernel, nt, ne),
        out_shape=jax.ShapeDtypeStruct(x.shape, F32),
        in_specs=[vmem],
        out_specs=vmem,
        scratch_shapes=[VMEM((width // LANES, per, lr, LANES), F32), dma((ne,)), dma((ne,))],
        compiler_params=pltpu.CompilerParams(collective_id=2, has_side_effects=True),
        name="spread",
    )(cols.reshape(pieces, members, lr, LANES))


def solution(mesh):
    in_specs = (
        P("ens", None, "tile", None),
        P(None, None, "tile", None),
        P(None, None, "tile"),
        P(None, "tile"),
        P(None, "tile"),
        P(None, "tile"),
    )
    out_specs = P("ens", None, "tile", None)
    body = functools.partial(on_device, mesh.shape["tile"], mesh.shape["ens"])
    return jax.shard_map(body, mesh=mesh, in_specs=in_specs, out_specs=out_specs, check_vma=False)
```

```python
import functools

import jax
import jax.numpy as jnp
from jax import lax
from jax.experimental import pallas as pl
from jax.experimental.pallas import tpu as pltpu
from jax.sharding import PartitionSpec as P

BATCHES = 2
REACH = 2
WINDOW = 2 * REACH + 1
SPREAD_RATE = 0.05
EPSILON = 1e-06
MESH = pl.DeviceIdType.MESH
VMEM = pltpu.VMEM
LANES = 128
BLOCK = 256
FORWARD_RIGHT = (2, 1, 3)
ORDER = (2, 1, 3, 0, 4)
F32 = jnp.float32
BF16 = jnp.bfloat16


def rdma(src, dst, send_sem, recv_sem, device):
    return pltpu.make_async_remote_copy(
        src_ref=src,
        dst_ref=dst,
        send_sem=send_sem,
        recv_sem=recv_sem,
        device_id=device,
        device_id_type=MESH,
    )


def greet(devices):
    barrier = pltpu.get_barrier_semaphore()
    for device in devices:
        pl.semaphore_signal(barrier, inc=1, device_id=device, device_id_type=MESH)
    pl.semaphore_wait(barrier, len(devices))


def split2(value):
    high = value.astype(BF16).astype(F32)
    return high, value - high


class Exchange:
    def __init__(self, gathered, send, recv, t, e, nt, ne):
        self.gathered, self.send, self.recv = gathered, send, recv
        self.t, self.e, self.nt = t, e, nt
        self.right, self.left = lax.rem(e + 2, ne), lax.rem(e + ne - 2, ne)
        self.partner = e + 1 - 2 * lax.rem(e, 2)
        self.slots = [
            e,
            self.left,
            self.right,
            lax.rem(e + 4, ne),
            self.partner,
            lax.rem(self.partner + ne - 2, ne),
            lax.rem(self.partner + 2, ne),
            lax.rem(self.partner + 4, ne),
        ]
        self.started = []

    def go(self, k, rel, target_k, target_rel, device):
        copy = rdma(
            self.gathered.at[k, self.slots[rel]],
            self.gathered.at[target_k, self.slots[rel]],
            self.send.at[len(self.started)],
            self.recv.at[target_k, target_rel],
            device,
        )
        copy.start()
        self.started.append(copy)

    def arrive(self, k, rel):
        rdma(
            self.gathered.at[k, self.slots[rel]],
            self.gathered.at[k, self.slots[rel]],
            self.send.at[0],
            self.recv.at[k, rel],
            (self.t, self.partner),
        ).wait_recv()

    def along(self, k):
        self.go(k, 0, k, 1, (self.t, self.right))
        self.go(k, 0, k, 2, (self.t, self.left))
        self.go(k, 0, k, 4, (self.t, self.partner))

    def start(self):
        for offset in (1, -1, 2, -2):
            tile = lax.rem(self.t + self.nt + offset, self.nt)
            self.go(REACH, 0, REACH - offset, 0, (tile, self.e))
        self.along(REACH)

    def tiles(self, ks):
        for k in ks:
            self.arrive(k, 0)
            self.along(k)

    def sides(self, k):
        self.arrive(k, 1)
        if k in FORWARD_RIGHT:
            self.go(k, 1, k, 3, (self.t, self.right))
        self.go(k, 1, k, 5, (self.t, self.partner))
        self.arrive(k, 2)
        if k not in FORWARD_RIGHT:
            self.go(k, 2, k, 3, (self.t, self.left))
        self.go(k, 2, k, 6, (self.t, self.partner))

    def far(self, k):
        self.arrive(k, 3)
        self.go(k, 3, k, 7, (self.t, self.partner))

    def finish(self, k):
        for rel in (4, 5, 6, 7):
            self.arrive(k, rel)


EXCHANGE_SENDS = 4 + 3 * WINDOW + 3 * WINDOW + WINDOW


def tile_peers(t, e, nt):
    return [(lax.rem(t + nt + offset, nt), e) for offset in (1, -1, 2, -2)]


def ens_peers(t, e, ne):
    return [(t, lax.rem(e + d, ne)) for d in range(1, ne)]


def cycle_kernel(
    nt, ne,
    x, u, loc, cnt, val, err, out,
    first, later, cols, meta, grid,
    hs, hr, tmp, ub, bg, parts, sb, rb, second,
    weights, shifts, states, total, closes, gains, ahead,
    halo_s, halo_r, meta_s, meta_r, bulk_s, bulk_r, small_s, small_r,
    first_s, first_r, later_s, later_r, out_s, out_r, own_sem,
):
    t, e = lax.axis_index("tile"), lax.axis_index("ens")
    per, levels, rows, width = x.shape
    lr = levels * rows
    col_count = width // ne
    slots = loc.shape[2]

    def fill(m, carry):
        for l in range(levels):
            hs[0, m, l : l + 1, :] = x[m, l, 0:1, :]
            hs[1, m, l : l + 1, :] = x[m, l, rows - 1 : rows, :]
        return carry

    lax.fori_loop(0, per, fill, 0)
    slot_index = lax.broadcasted_iota(jnp.int32, (1, slots), 1)
    for b in range(BATCHES):
        for i in range(3):
            meta[REACH, b, i : i + 1, :] = loc[i, b : b + 1, :].astype(F32)
        meta[REACH, b, 3:4, :] = val[b : b + 1, :]
        meta[REACH, b, 4:5, :] = err[b : b + 1, :]
        meta[REACH, b, 5:6, :] = (slot_index < cnt[0:1, b : b + 1]).astype(F32)
        meta[REACH, b, 6:8, :] = jnp.zeros((2, slots), F32)
    greet(tile_peers(t, e, nt) + ens_peers(t, e, ne))
    up_tile, down_tile = lax.rem(t + nt - 1, nt), lax.rem(t + 1, nt)
    halos = [
        rdma(hs.at[1], hr.at[0], halo_s.at[0], halo_r.at[0], (down_tile, e)),
        rdma(hs.at[0], hr.at[1], halo_s.at[1], halo_r.at[1], (up_tile, e)),
    ]
    for copy in halos:
        copy.start()
    metas = []
    for i, offset in enumerate((1, -1, 2, -2)):
        copy = rdma(
            meta.at[REACH],
            meta.at[REACH - offset],
            meta_s.at[i],
            meta_r.at[i],
            (lax.rem(t + nt + offset, nt), e),
        )
        copy.start()
        metas.append(copy)
    for a in range(2):
        for l in range(levels):
            ub[a, l * rows : (l + 1) * rows, :] = u[a, l]
    for copy in halos:
        copy.wait_recv()
    has_up = jnp.where(t > 0, 1.0, 0.0).astype(F32)
    has_down = jnp.where(t < nt - 1, 1.0, 0.0).astype(F32)

    def step(m, carry):
        for l in range(levels):
            tmp[l * rows : (l + 1) * rows, :] = x[m, l]
        c = tmp[...]
        above = hr[0, m] * has_up
        below = hr[1, m] * has_down
        row = lax.broadcasted_iota(jnp.int32, (lr, width), 0)
        col = lax.broadcasted_iota(jnp.int32, (lr, width), 1)
        up = pltpu.roll(c, 1, 0)
        down = pltpu.roll(c, lr - 1, 0)
        for l in range(levels):
            up = jnp.where(row == l * rows, above[l : l + 1], up)
            down = jnp.where(row == l * rows + rows - 1, below[l : l + 1], down)
        west = jnp.where(col == 0, 0.0, pltpu.roll(c, 1, 1))
        east = jnp.where(col == width - 1, 0.0, pltpu.roll(c, width - 1, 1))
        wr, wc = ub[0], ub[1]
        tendency = (
            jnp.maximum(wr, 0.0) * (c - up)
            + jnp.minimum(wr, 0.0) * (down - c)
            + jnp.maximum(wc, 0.0) * (c - west)
            + jnp.minimum(wc, 0.0) * (east - c)
        )
        value = c - tendency + SPREAD_RATE * (up + down + west + east - 4.0 * c)
        for i in range(width // LANES):
            bg[i, pl.ds(m * lr, lr), :] = value[:, i * LANES : (i + 1) * LANES]
        return carry

    lax.fori_loop(0, per, step, 0)

    pieces = col_count // LANES

    def block_of(device):
        return pl.ds(device * pieces, pieces)

    def members_of(device):
        return pl.ds(pl.multiple_of(device * per * lr, per * lr), per * lr)

    bulks = []

    def send_bulk(d):
        peer = lax.rem(e + d, ne)
        copy = rdma(
            bg.at[block_of(peer)],
            cols.at[:, members_of(e)],
            bulk_s.at[d],
            bulk_r.at[d],
            (t, peer),
        )
        copy.start()
        bulks.append(copy)

    own = pltpu.make_async_copy(bg.at[block_of(e)], cols.at[:, members_of(e)], own_sem)
    own.start()
    for d in (1, 2, ne - 1, ne - 2):
        send_bulk(d)

    def split(kk, carry):
        f = jnp.concatenate([bg[2 * kk], bg[2 * kk + 1]], axis=1)
        high, rest = split2(f)
        middle, low = split2(rest)
        parts[kk] = jnp.concatenate([high, middle, low], axis=0).astype(BF16)
        return carry

    lax.fori_loop(0, width // BLOCK, split, 0)
    held = per * lr
    for b in range(BATCHES):

        def pick(j, carry):
            here = pl.ds(pl.multiple_of(j * BLOCK, BLOCK), BLOCK)
            place = loc[2, b : b + 1, here] * rows + (loc[0, b : b + 1, here] - t * rows)
            column = loc[1, b : b + 1, here]
            down = lax.broadcasted_iota(jnp.int32, (BLOCK, BLOCK), 0)
            total = jnp.zeros((3 * held, BLOCK), F32)
            for kk in range(width // BLOCK):
                hot = jnp.where(down == column - kk * BLOCK, 1.0, 0.0).astype(BF16)
                total += jnp.dot(parts[kk], hot, preferred_element_type=F32)
            value = total[0:held] + total[held : 2 * held] + total[2 * held :]
            mine = lax.broadcasted_iota(jnp.int32, (lr, BLOCK), 0) == place
            value = jnp.where(mine[None], value.reshape(per, lr, BLOCK), 0.0)
            value = jnp.sum(value, axis=1)
            for half in range(BLOCK // LANES):
                sb[j * (BLOCK // LANES) + half, b, 0:per, :] = value[
                    :, half * LANES : (half + 1) * LANES
                ]
            return carry

        lax.fori_loop(0, slots // BLOCK, pick, 0)

    smalls = []
    for d in (4, 3, 5, 2, 6, 1, 7):
        peer = lax.rem(e + d, ne)
        copy = rdma(sb.at[peer], rb.at[e], small_s.at[d], small_r.at[d], (t, peer))
        copy.start()
        smalls.append(copy)
    for d in (4, 3, 5):
        send_bulk(d)
    rb[e] = sb[e]
    for d in range(1, ne):
        source = lax.rem(e + ne - d, ne)
        rdma(
            sb.at[source], rb.at[source], small_s.at[d], small_r.at[d], (t, source)
        ).wait_recv()
    for s in range(ne):
        first[REACH, e, s * per : (s + 1) * per, :] = rb[s, 0, 0:per, :]
        second[s * per : (s + 1) * per, :] = rb[s, 1, 0:per, :]
    members = per * ne
    halves = pieces
    width = col_count
    span = rows * width
    slot_blocks = slots // BLOCK
    exchanges = [
        Exchange(first, first_s, first_r, t, e, nt, ne),
        Exchange(later, later_s, later_r, t, e, nt, ne),
    ]
    inverse_col = 1.0 / float(x.shape[3] // 2)
    inverse_row = 1.0 / float(REACH * rows)

    def prepare(k, batch):
        gathered = exchanges[batch].gathered

        def piece(s, inner):
            here = pl.ds(pl.multiple_of(s * BLOCK, BLOCK), BLOCK)
            p = jnp.concatenate([gathered[k, 2 * s], gathered[k, 2 * s + 1]], axis=1)
            lev = meta[k, batch, 2:3, here]
            value = meta[k, batch, 3:4, here]
            error = meta[k, batch, 4:5, here]
            live = meta[k, batch, 5:6, here]
            average = jnp.sum(p, axis=0, keepdims=True) / members
            deviation = p - average
            variance = (
                jnp.sum(deviation * deviation, axis=0, keepdims=True) / (members - 1) + EPSILON
            )
            combined = variance + error
            shrink = jnp.sqrt(error / combined)
            mean_post = (error * average + variance * value) / combined
            shift = live * ((shrink - 1.0) * deviation + (mean_post - average))
            weight = deviation * (live / ((members - 1) * variance))
            high, low = split2(weight)
            for l in range(levels):
                factor = jnp.where(lev == float(l), 1.0, 0.5)
                scaled = (high * factor).astype(BF16)
                weights[k, l, 0:members, here] = scaled
                weights[k, l, members : 2 * members, here] = scaled
                weights[k, l, 2 * members : 3 * members, here] = (low * factor).astype(BF16)
            both = jnp.concatenate(split2(shift), axis=0)
            shifts[k, here, :] = both.T.astype(BF16)
            return inner

        lax.fori_loop(0, slot_blocks, piece, 0)

    def cell_major(value):
        high, low = split2(value)
        return jnp.concatenate([high, low, high], axis=0).T.astype(BF16)

    def member_major(value):
        turned = value.T
        return turned[0:members] + turned[members : 2 * members]

    def load_states():
        for i in range(lr):
            here = pl.ds(i, members, stride=lr)
            value = jnp.concatenate([cols[h, here, :] for h in range(halves)], axis=1)
            states[i // rows, i % rows * width : (i % rows + 1) * width, :] = cell_major(value)
        total[...] = jnp.zeros_like(total)

    def store_states():
        for i in range(lr):
            here = pl.ds(i, members, stride=lr)
            change = member_major(total[i * width : (i + 1) * width, :])
            for h in range(halves):
                cols[h, here, :] = cols[h, here, :] + change[:, h * LANES : (h + 1) * LANES]

    def split_gain(gain):
        high = gain.astype(BF16)
        low = (gain - high.astype(F32)).astype(BF16)
        return jnp.concatenate([high, low], axis=1)

    def doubled(k, here):
        right = shifts[k, here, :]
        return jnp.concatenate([right, right], axis=0)

    def look():
        mine = pl.ds(pl.multiple_of(e * LANES, LANES), LANES)
        places = meta[REACH, 1, :, mine].T
        cell_row, cell_col, cell_lev = places[:, 0:1], places[:, 1:2], places[:, 2:3]
        x2 = cell_major(second[...])
        ahead[...] = jnp.zeros_like(ahead)
        for k in range(WINDOW):

            def block(j, inner):
                here = pl.ds(pl.multiple_of(j * BLOCK, BLOCK), BLOCK)
                row_gap = (cell_row - meta[k, 0, 0:1, here]) * inverse_row
                col_gap = (cell_col - meta[k, 0, 1:2, here]) * inverse_col
                close = jnp.maximum(1.0 - row_gap * row_gap - col_gap * col_gap, 0.0)
                low = jnp.dot(x2, weights[k, 0, :, here], preferred_element_type=F32)
                high = jnp.dot(x2, weights[k, 1, :, here], preferred_element_type=F32)
                gain = jnp.where(cell_lev == 0.0, low, high) * (close * close)
                ahead[...] += jnp.dot(
                    split_gain(gain), doubled(k, here), preferred_element_type=F32
                )
                return inner

            lax.fori_loop(0, slot_blocks, block, 0)
        later[REACH, e] = second[...] + member_major(ahead[...])

    def update(k, batch):
        first_cell = 1 if k == 2 * REACH else 0
        last_cell = rows - 1 if k == 0 else rows
        from_cell, to_cell = first_cell * width, last_cell * width
        cells = to_cell - from_cell

        def block(j, inner):
            here = pl.ds(pl.multiple_of(j * BLOCK, BLOCK), BLOCK)
            cell_col = (
                lax.broadcasted_iota(jnp.int32, (width, BLOCK), 0) + e * width
            ).astype(F32) * inverse_col
            col_gap = cell_col - meta[k, batch, 1:2, here] * inverse_col
            col_part = col_gap * col_gap
            obs_row = meta[k, batch, 0:1, here]
            for r in range(first_cell, last_cell):
                row_gap = ((t * rows + r).astype(F32) - obs_row) * inverse_row
                close = jnp.maximum((1.0 - row_gap * row_gap) - col_part, 0.0)
                closes[r * width : (r + 1) * width, :] = close * close
            for l in range(levels):
                covariance = jnp.dot(
                    states[l, from_cell:to_cell, :],
                    weights[k, l, :, here],
                    preferred_element_type=F32,
                )
                gains[l * cells : (l + 1) * cells, :] = split_gain(
                    covariance * closes[from_cell:to_cell, :]
                )
            change = jnp.dot(
                gains[0 : levels * cells, :], doubled(k, here), preferred_element_type=F32
            )
            for l in range(levels):
                total[l * span + from_cell : l * span + to_cell, :] += change[
                    l * cells : (l + 1) * cells
                ]
            return inner

        lax.fori_loop(0, slot_blocks, block, 0)

    now, then = exchanges
    now.start()
    now.tiles((1, 3, 0, 4))
    own.wait()
    for d in range(1, ne):
        source = lax.rem(e + ne - d, ne)
        rdma(
            bg.at[block_of(source)],
            cols.at[:, members_of(source)],
            bulk_s.at[d],
            bulk_r.at[d],
            (t, source),
        ).wait_recv()
    for i, offset in enumerate((1, -1, 2, -2)):
        rdma(
            meta.at[REACH],
            meta.at[REACH - offset],
            meta_s.at[i],
            meta_r.at[i],
            (up_tile, e),
        ).wait_recv()
    load_states()
    now.sides(2)
    now.sides(1)
    now.sides(3)
    now.far(2)
    now.finish(2)
    prepare(2, 0)
    update(2, 0)
    now.sides(0)
    now.sides(4)
    now.far(1)
    now.far(3)
    now.finish(1)
    prepare(1, 0)
    now.far(0)
    now.far(4)
    update(1, 0)
    for k in (3, 0, 4):
        now.finish(k)
        prepare(k, 0)
    look()
    then.start()
    update(3, 0)
    then.tiles((1, 3, 0, 4))
    update(0, 0)
    then.sides(2)
    then.sides(1)
    then.sides(3)
    update(4, 0)
    store_states()
    load_states()
    then.far(2)
    then.sides(0)
    then.sides(4)
    then.finish(2)
    prepare(2, 1)
    then.far(1)
    then.far(3)
    update(2, 1)
    then.far(0)
    then.far(4)
    for k in (1, 3, 0, 4):
        then.finish(k)
        prepare(k, 1)
        update(k, 1)
    store_states()
    copies = []
    for d in (4, 3, 5, 2, 6, 1, 7):
        peer = lax.rem(e + d, ne)
        copy = rdma(
            cols.at[:, members_of(peer)],
            grid.at[block_of(e)],
            out_s.at[d],
            out_r.at[d],
            (t, peer),
        )
        copy.start()
        copies.append(copy)
    home = pltpu.make_async_copy(cols.at[:, members_of(e)], grid.at[block_of(e)], out_s.at[0])
    home.start()
    home.wait()
    for d in range(1, ne):
        source = lax.rem(e + ne - d, ne)
        rdma(
            cols.at[:, members_of(source)],
            grid.at[block_of(source)],
            out_s.at[d],
            out_r.at[d],
            (t, source),
        ).wait_recv()

    def put(m, carry):
        for l in range(levels):
            for i in range(x.shape[3] // LANES):
                out[m, l, :, i * LANES : (i + 1) * LANES] = grid[
                    i, pl.ds(m * lr + l * rows, rows), :
                ]
        return carry

    lax.fori_loop(0, per, put, 0)
    for copy in halos + metas + bulks + smalls + copies + now.started + then.started:
        copy.wait_send()


def on_device(nt, ne, x, u, loc, cnt, val, err):
    per, levels, rows, width = x.shape
    lr = levels * rows
    members = per * ne
    slots = val.shape[1]
    col_count = width // ne
    vmem = pl.BlockSpec(memory_space=VMEM)
    dma = pltpu.SemaphoreType.DMA
    window = VMEM((WINDOW, ne, members, LANES), F32)
    whole = VMEM((width // LANES, per * lr, LANES), F32)
    return pl.pallas_call(
        functools.partial(cycle_kernel, nt, ne),
        out_shape=jax.ShapeDtypeStruct(x.shape, F32),
        in_specs=[vmem] * 6,
        out_specs=vmem,
        scratch_shapes=[
            window,
            window,
            VMEM((col_count // LANES, members * lr, LANES), F32),
            VMEM((WINDOW, BATCHES, 8, slots), F32),
            whole,
            VMEM((2, per, levels, width), F32),
            VMEM((2, per, levels, width), F32),
            VMEM((lr, width), F32),
            VMEM((2, lr, width), F32),
            whole,
            VMEM((width // BLOCK, 3 * per * lr, BLOCK), BF16),
            VMEM((ne, BATCHES, 16, LANES), F32),
            VMEM((ne, BATCHES, 16, LANES), F32),
            VMEM((members, LANES), F32),
            VMEM((WINDOW, levels, 3 * members, slots), BF16),
            VMEM((WINDOW, slots, 2 * members), BF16),
            VMEM((levels, rows * col_count, 3 * members), BF16),
            VMEM((lr * col_count, 2 * members), F32),
            VMEM((rows * col_count, BLOCK), F32),
            VMEM((lr * col_count, 2 * BLOCK), BF16),
            VMEM((LANES, 2 * members), F32),
            dma((2,)),
            dma((2,)),
            dma((4,)),
            dma((4,)),
            dma((ne,)),
            dma((ne,)),
            dma((ne,)),
            dma((ne,)),
            dma((EXCHANGE_SENDS,)),
            dma((WINDOW, ne)),
            dma((EXCHANGE_SENDS,)),
            dma((WINDOW, ne)),
            dma((ne,)),
            dma((ne,)),
            dma,
        ],
        compiler_params=pltpu.CompilerParams(collective_id=0, has_side_effects=True),
        name="cycle",
    )(x, u, loc, cnt.T, val, err)


def solution(mesh):
    in_specs = (
        P("ens", None, "tile", None),
        P(None, None, "tile", None),
        P(None, None, "tile"),
        P(None, "tile"),
        P(None, "tile"),
        P(None, "tile"),
    )
    out_specs = P("ens", None, "tile", None)
    body = functools.partial(on_device, mesh.shape["tile"], mesh.shape["ens"])
    return jax.shard_map(body, mesh=mesh, in_specs=in_specs, out_specs=out_specs, check_vma=False)
```

```python
import functools

import jax
import jax.numpy as jnp
from jax import lax
from jax.experimental import pallas as pl
from jax.experimental.pallas import tpu as pltpu
from jax.sharding import PartitionSpec as P

BATCHES = 2
REACH = 2
WINDOW = 2 * REACH + 1
SPREAD_RATE = 0.05
EPSILON = 1e-06
MESH = pl.DeviceIdType.MESH
VMEM = pltpu.VMEM
LANES = 128
BLOCK = 256
FORWARD_RIGHT = (2, 1, 3)
ORDER = (2, 1, 3, 0, 4)
F32 = jnp.float32
BF16 = jnp.bfloat16


def rdma(src, dst, send_sem, recv_sem, device):
    return pltpu.make_async_remote_copy(
        src_ref=src,
        dst_ref=dst,
        send_sem=send_sem,
        recv_sem=recv_sem,
        device_id=device,
        device_id_type=MESH,
    )


def greet(devices):
    barrier = pltpu.get_barrier_semaphore()
    for device in devices:
        pl.semaphore_signal(barrier, inc=1, device_id=device, device_id_type=MESH)
    pl.semaphore_wait(barrier, len(devices))


def split2(value):
    high = value.astype(BF16).astype(F32)
    return high, value - high


class Exchange:
    def __init__(self, gathered, send, recv, t, e, nt, ne):
        self.gathered, self.send, self.recv = gathered, send, recv
        self.t, self.e, self.nt = t, e, nt
        self.right, self.left = lax.rem(e + 2, ne), lax.rem(e + ne - 2, ne)
        self.partner = e + 1 - 2 * lax.rem(e, 2)
        self.slots = [
            e,
            self.left,
            self.right,
            lax.rem(e + 4, ne),
            self.partner,
            lax.rem(self.partner + ne - 2, ne),
            lax.rem(self.partner + 2, ne),
            lax.rem(self.partner + 4, ne),
        ]
        self.started = []

    def go(self, k, rel, target_k, target_rel, device):
        copy = rdma(
            self.gathered.at[k, self.slots[rel]],
            self.gathered.at[target_k, self.slots[rel]],
            self.send.at[len(self.started)],
            self.recv.at[target_k, target_rel],
            device,
        )
        copy.start()
        self.started.append(copy)

    def arrive(self, k, rel):
        rdma(
            self.gathered.at[k, self.slots[rel]],
            self.gathered.at[k, self.slots[rel]],
            self.send.at[0],
            self.recv.at[k, rel],
            (self.t, self.partner),
        ).wait_recv()

    def along(self, k):
        self.go(k, 0, k, 1, (self.t, self.right))
        self.go(k, 0, k, 2, (self.t, self.left))
        self.go(k, 0, k, 4, (self.t, self.partner))

    def start(self):
        for offset in (1, -1, 2, -2):
            tile = lax.rem(self.t + self.nt + offset, self.nt)
            self.go(REACH, 0, REACH - offset, 0, (tile, self.e))
        self.along(REACH)

    def tiles(self, ks):
        for k in ks:
            self.arrive(k, 0)
            self.along(k)

    def sides(self, k):
        self.arrive(k, 1)
        if k in FORWARD_RIGHT:
            self.go(k, 1, k, 3, (self.t, self.right))
        self.go(k, 1, k, 5, (self.t, self.partner))
        self.arrive(k, 2)
        if k not in FORWARD_RIGHT:
            self.go(k, 2, k, 3, (self.t, self.left))
        self.go(k, 2, k, 6, (self.t, self.partner))

    def far(self, k):
        self.arrive(k, 3)
        self.go(k, 3, k, 7, (self.t, self.partner))

    def finish(self, k):
        for rel in (4, 5, 6, 7):
            self.arrive(k, rel)


EXCHANGE_SENDS = 4 + 3 * WINDOW + 3 * WINDOW + WINDOW


def tile_peers(t, e, nt):
    return [(lax.rem(t + nt + offset, nt), e) for offset in (1, -1, 2, -2)]


def ens_peers(t, e, ne):
    return [(t, lax.rem(e + d, ne)) for d in range(1, ne)]


def cycle_kernel(
    nt, ne,
    x, u, loc, cnt, val, err, out,
    first, later, cols, meta, leaving, grid,
    hs, hr, tmp, ub, bg, parts, sb, rb, second, x2,
    weights, shifts, states, total, closes, gains, ahead,
    halo_s, halo_r, meta_s, meta_r, bulk_s, bulk_r, small_s, small_r,
    first_s, first_r, later_s, later_r, out_s, out_r, own_sem,
):
    t, e = lax.axis_index("tile"), lax.axis_index("ens")
    per, levels, rows, width = x.shape
    lr = levels * rows
    col_count = width // ne
    slots = loc.shape[2]

    def fill(m, carry):
        for l in range(levels):
            hs[0, m, l : l + 1, :] = x[m, l, 0:1, :]
            hs[1, m, l : l + 1, :] = x[m, l, rows - 1 : rows, :]
        return carry

    lax.fori_loop(0, per, fill, 0)
    slot_index = lax.broadcasted_iota(jnp.int32, (1, slots), 1)
    for b in range(BATCHES):
        for i in range(3):
            meta[REACH, b, i : i + 1, :] = loc[i, b : b + 1, :].astype(F32)
        meta[REACH, b, 3:4, :] = val[b : b + 1, :]
        meta[REACH, b, 4:5, :] = err[b : b + 1, :]
        meta[REACH, b, 5:6, :] = (slot_index < cnt[0:1, b : b + 1]).astype(F32)
        meta[REACH, b, 6:8, :] = jnp.zeros((2, slots), F32)
    greet(tile_peers(t, e, nt) + ens_peers(t, e, ne))
    up_tile, down_tile = lax.rem(t + nt - 1, nt), lax.rem(t + 1, nt)
    halos = [
        rdma(hs.at[1], hr.at[0], halo_s.at[0], halo_r.at[0], (down_tile, e)),
        rdma(hs.at[0], hr.at[1], halo_s.at[1], halo_r.at[1], (up_tile, e)),
    ]
    for copy in halos:
        copy.start()
    metas = []
    for i, offset in enumerate((1, -1, 2, -2)):
        copy = rdma(
            meta.at[REACH],
            meta.at[REACH - offset],
            meta_s.at[i],
            meta_r.at[i],
            (lax.rem(t + nt + offset, nt), e),
        )
        copy.start()
        metas.append(copy)
    for a in range(2):
        for l in range(levels):
            ub[a, l * rows : (l + 1) * rows, :] = u[a, l]
    for copy in halos:
        copy.wait_recv()
    has_up = jnp.where(t > 0, 1.0, 0.0).astype(F32)
    has_down = jnp.where(t < nt - 1, 1.0, 0.0).astype(F32)

    def step(m, carry):
        for l in range(levels):
            tmp[l * rows : (l + 1) * rows, :] = x[m, l]
        c = tmp[...]
        above = hr[0, m] * has_up
        below = hr[1, m] * has_down
        row = lax.broadcasted_iota(jnp.int32, (lr, width), 0)
        col = lax.broadcasted_iota(jnp.int32, (lr, width), 1)
        up = pltpu.roll(c, 1, 0)
        down = pltpu.roll(c, lr - 1, 0)
        for l in range(levels):
            up = jnp.where(row == l * rows, above[l : l + 1], up)
            down = jnp.where(row == l * rows + rows - 1, below[l : l + 1], down)
        west = jnp.where(col == 0, 0.0, pltpu.roll(c, 1, 1))
        east = jnp.where(col == width - 1, 0.0, pltpu.roll(c, width - 1, 1))
        wr, wc = ub[0], ub[1]
        tendency = (
            jnp.maximum(wr, 0.0) * (c - up)
            + jnp.minimum(wr, 0.0) * (down - c)
            + jnp.maximum(wc, 0.0) * (c - west)
            + jnp.minimum(wc, 0.0) * (east - c)
        )
        value = c - tendency + SPREAD_RATE * (up + down + west + east - 4.0 * c)
        for i in range(width // LANES):
            bg[i, pl.ds(m * lr, lr), :] = value[:, i * LANES : (i + 1) * LANES]
        return carry

    lax.fori_loop(0, per, step, 0)

    pieces = col_count // LANES

    def block_of(device):
        return pl.ds(device * pieces, pieces)

    def members_of(device):
        return pl.ds(pl.multiple_of(device * per * lr, per * lr), per * lr)

    bulks = []

    def send_bulk(d):
        peer = lax.rem(e + d, ne)
        copy = rdma(
            bg.at[block_of(peer)],
            cols.at[:, members_of(e)],
            bulk_s.at[d],
            bulk_r.at[d],
            (t, peer),
        )
        copy.start()
        bulks.append(copy)

    own = pltpu.make_async_copy(bg.at[block_of(e)], cols.at[:, members_of(e)], own_sem)
    own.start()
    for d in (1, 2, ne - 1, ne - 2):
        send_bulk(d)

    def split(kk, carry):
        f = jnp.concatenate([bg[2 * kk], bg[2 * kk + 1]], axis=1)
        high, rest = split2(f)
        middle, low = split2(rest)
        parts[kk] = jnp.concatenate([high, middle, low], axis=0).astype(BF16)
        return carry

    lax.fori_loop(0, width // BLOCK, split, 0)
    held = per * lr
    def pick(b, j):
        here = slice(j * BLOCK, (j + 1) * BLOCK)
        place = loc[2, b : b + 1, here] * rows + (loc[0, b : b + 1, here] - t * rows)
        column = loc[1, b : b + 1, here]
        down = lax.broadcasted_iota(jnp.int32, (BLOCK, BLOCK), 0)
        picked = jnp.zeros((3 * held, BLOCK), F32)
        for kk in range(x.shape[3] // BLOCK):
            hot = jnp.where(down == column - kk * BLOCK, 1.0, 0.0).astype(BF16)
            picked += jnp.dot(parts[kk], hot, preferred_element_type=F32)
        value = picked[0:held] + picked[held : 2 * held] + picked[2 * held :]
        mine = lax.broadcasted_iota(jnp.int32, (lr, BLOCK), 0) == place
        value = jnp.where(mine[None], value.reshape(per, lr, BLOCK), 0.0)
        value = jnp.sum(value, axis=1)
        for half in range(BLOCK // LANES):
            i = j * (BLOCK // LANES) + half
            part = value[:, half * LANES : (half + 1) * LANES]
            if b == 0:
                first[REACH, e, i * per : (i + 1) * per, :] = part
            else:
                sb[i, 0:per, :] = part

    members = per * ne
    halves = pieces
    width = col_count
    span = rows * width
    slot_blocks = slots // BLOCK
    exchanges = [
        Exchange(first, first_s, first_r, t, e, nt, ne),
        Exchange(later, later_s, later_r, t, e, nt, ne),
    ]
    inverse_col = 1.0 / float(x.shape[3] // 2)
    inverse_row = 1.0 / float(REACH * rows)

    def prior_of(k, batch, s):
        if batch:
            return jnp.concatenate([later[k, 2 * s], later[k, 2 * s + 1]], axis=1)
        return jnp.concatenate(
            [
                jnp.concatenate(
                    [first[k, d, i * per : (i + 1) * per, :] for d in range(ne)], axis=0
                )
                for i in (2 * s, 2 * s + 1)
            ],
            axis=1,
        )

    def prepare(k, batch):
        for s in range(slot_blocks):
            here = slice(s * BLOCK, (s + 1) * BLOCK)
            p = prior_of(k, batch, s)
            lev = meta[k, batch, 2:3, here]
            value = meta[k, batch, 3:4, here]
            error = meta[k, batch, 4:5, here]
            live = meta[k, batch, 5:6, here]
            average = jnp.sum(p, axis=0, keepdims=True) / members
            deviation = p - average
            variance = (
                jnp.sum(deviation * deviation, axis=0, keepdims=True) / (members - 1) + EPSILON
            )
            combined = variance + error
            shrink = jnp.sqrt(error / combined)
            mean_post = (error * average + variance * value) / combined
            shift = live * ((shrink - 1.0) * deviation + (mean_post - average))
            weight = deviation * (live / ((members - 1) * variance))
            high, low = split2(weight)
            for l in range(levels):
                factor = jnp.where(lev == float(l), 1.0, 0.5)
                scaled = (high * factor).astype(BF16)
                weights[k, l, 0:members, here] = scaled
                weights[k, l, members : 2 * members, here] = scaled
                weights[k, l, 2 * members : 3 * members, here] = (low * factor).astype(BF16)
            both = jnp.concatenate(split2(shift), axis=0)
            shifts[k, here, :] = both.T.astype(BF16)

    def cell_major(value):
        high, low = split2(value)
        return jnp.concatenate([high, low, high], axis=0).T.astype(BF16)

    def member_major(value):
        turned = value.T
        return turned[0:members] + turned[members : 2 * members]

    def load_states():
        for i in range(lr):
            here = pl.ds(i, members, stride=lr)
            value = jnp.concatenate([cols[h, here, :] for h in range(halves)], axis=1)
            states[i // rows, i % rows * width : (i % rows + 1) * width, :] = cell_major(value)
        total[...] = jnp.zeros_like(total)

    def part_of(device):
        return pl.ds(pl.multiple_of(device * per * rows, per * rows), per * rows)

    def store_states():
        for i in range(lr):
            here = pl.ds(i, members, stride=lr)
            change = member_major(total[i * width : (i + 1) * width, :])
            for h in range(halves):
                cols[h, here, :] = cols[h, here, :] + change[:, h * LANES : (h + 1) * LANES]

    def split_gain(gain):
        high = gain.astype(BF16)
        low = (gain - high.astype(F32)).astype(BF16)
        return jnp.concatenate([high, low], axis=1)

    def doubled(k, here):
        right = shifts[k, here, :]
        return jnp.concatenate([right, right], axis=0)

    def look(k):
        mine = pl.ds(pl.multiple_of(e * LANES, LANES), LANES)
        places = meta[REACH, 1, :, mine].T
        cell_row, cell_col, cell_lev = places[:, 0:1], places[:, 1:2], places[:, 2:3]

        def block(j, inner):
            here = pl.ds(pl.multiple_of(j * BLOCK, BLOCK), BLOCK)
            row_gap = (cell_row - meta[k, 0, 0:1, here]) * inverse_row
            col_gap = (cell_col - meta[k, 0, 1:2, here]) * inverse_col
            close = jnp.maximum(1.0 - row_gap * row_gap - col_gap * col_gap, 0.0)
            factor = jnp.where(meta[k, 0, 2:3, here] == 0.0, 0.5, 2.0)
            factor = jnp.where(cell_lev == 0.0, 1.0, factor)
            gain = jnp.dot(x2[...], weights[k, 0, :, here], preferred_element_type=F32)
            gain = gain * (close * close * factor)
            ahead[...] += jnp.dot(split_gain(gain), doubled(k, here), preferred_element_type=F32)
            return inner

        lax.fori_loop(0, slot_blocks, block, 0)

    def update(k, batch, chosen=(0, 1), start=0, stop=None):
        stop = slot_blocks if stop is None else stop
        first_cell = 1 if k == 2 * REACH else 0
        last_cell = rows - 1 if k == 0 else rows
        from_cell, to_cell = first_cell * width, last_cell * width
        cells = to_cell - from_cell

        def block(j, inner):
            here = pl.ds(pl.multiple_of(j * BLOCK, BLOCK), BLOCK)
            cell_col = (
                lax.broadcasted_iota(jnp.int32, (width, BLOCK), 0) + e * width
            ).astype(F32) * inverse_col
            col_gap = cell_col - meta[k, batch, 1:2, here] * inverse_col
            col_part = col_gap * col_gap
            obs_row = meta[k, batch, 0:1, here]
            for r in range(first_cell, last_cell):
                row_gap = ((t * rows + r).astype(F32) - obs_row) * inverse_row
                close = jnp.maximum((1.0 - row_gap * row_gap) - col_part, 0.0)
                closes[r * width : (r + 1) * width, :] = close * close
            for i, l in enumerate(chosen):
                covariance = jnp.dot(
                    states[l, from_cell:to_cell, :],
                    weights[k, l, :, here],
                    preferred_element_type=F32,
                )
                gains[i * cells : (i + 1) * cells, :] = split_gain(
                    covariance * closes[from_cell:to_cell, :]
                )
            change = jnp.dot(
                gains[0 : len(chosen) * cells, :], doubled(k, here), preferred_element_type=F32
            )
            for i, l in enumerate(chosen):
                total[l * span + from_cell : l * span + to_cell, :] += change[
                    i * cells : (i + 1) * cells
                ]
            return inner

        lax.fori_loop(start, stop, block, 0)

    now, then = exchanges
    for j in range(slot_blocks):
        pick(0, j)
    now.start()
    for d in (4, 3, 5):
        send_bulk(d)
    for j in range(slot_blocks):
        pick(1, j)
    smalls = []
    for d in (4, 3, 5, 2, 6, 1, 7):
        peer = lax.rem(e + d, ne)
        copy = rdma(sb.at[peer], rb.at[e], small_s.at[d], small_r.at[d], (t, peer))
        copy.start()
        smalls.append(copy)
    rb[e] = sb[e]
    now.tiles((1, 3))
    now.sides(2)
    now.tiles((0, 4))
    for d in range(1, ne):
        source = lax.rem(e + ne - d, ne)
        rdma(
            sb.at[source], rb.at[source], small_s.at[d], small_r.at[d], (t, source)
        ).wait_recv()
    for s in range(ne):
        second[s * per : (s + 1) * per, :] = rb[s, 0:per, :]
    x2[...] = cell_major(second[...])
    ahead[...] = jnp.zeros_like(ahead)
    now.far(2)
    own.wait()
    for d in range(1, ne):
        source = lax.rem(e + ne - d, ne)
        rdma(
            bg.at[block_of(source)],
            cols.at[:, members_of(source)],
            bulk_s.at[d],
            bulk_r.at[d],
            (t, source),
        ).wait_recv()
    for i, offset in enumerate((1, -1, 2, -2)):
        rdma(
            meta.at[REACH],
            meta.at[REACH - offset],
            meta_s.at[i],
            meta_r.at[i],
            (up_tile, e),
        ).wait_recv()
    load_states()
    now.finish(2)
    prepare(2, 0)
    look(2)
    update(2, 0, stop=slot_blocks // 2)
    now.sides(1)
    now.sides(3)
    update(2, 0, start=slot_blocks // 2)
    now.far(1)
    now.far(3)
    now.sides(0)
    now.sides(4)
    now.finish(1)
    prepare(1, 0)
    look(1)
    now.far(0)
    now.far(4)
    for k in (3, 0, 4):
        now.finish(k)
        prepare(k, 0)
        look(k)
    later[REACH, e] = second[...] + member_major(ahead[...])
    then.start()
    update(1, 0)
    then.tiles((1, 3, 0, 4))
    then.sides(2)
    update(3, 0)
    then.far(2)
    then.sides(1)
    then.sides(3)
    update(0, 0)
    then.sides(0)
    then.sides(4)
    then.far(1)
    then.far(3)
    update(4, 0)
    then.far(0)
    then.far(4)
    store_states()
    load_states()
    for k in (2, 1, 3):
        then.finish(k)
        prepare(k, 1)
        update(k, 1)
    for k in (0, 4):
        then.finish(k)
        prepare(k, 1)
    copies, homes = [], []
    for l in range(levels):
        update(0, 1, chosen=(l,))
        update(4, 1, chosen=(l,))
        for r in range(rows):
            change = member_major(total[(l * rows + r) * width : (l * rows + r + 1) * width, :])
            for h in range(halves):
                leaving[l, h, pl.ds(r, members, stride=rows), :] = (
                    cols[h, pl.ds(l * rows + r, members, stride=lr), :]
                    + change[:, h * LANES : (h + 1) * LANES]
                )
        for d in (4, 3, 5, 2, 6, 1, 7):
            peer = lax.rem(e + d, ne)
            copy = rdma(
                leaving.at[l, :, part_of(peer)],
                grid.at[l, block_of(e)],
                out_s.at[l, d],
                out_r.at[l, d],
                (t, peer),
            )
            copy.start()
            copies.append(copy)
        home = pltpu.make_async_copy(
            leaving.at[l, :, part_of(e)], grid.at[l, block_of(e)], out_s.at[l, 0]
        )
        home.start()
        homes.append(home)
    for l in range(levels):
        homes[l].wait()
        for d in range(1, ne):
            source = lax.rem(e + ne - d, ne)
            rdma(
                leaving.at[l, :, part_of(source)],
                grid.at[l, block_of(source)],
                out_s.at[l, d],
                out_r.at[l, d],
                (t, source),
            ).wait_recv()

    def put(m, carry):
        for l in range(levels):
            for i in range(x.shape[3] // LANES):
                out[m, l, :, i * LANES : (i + 1) * LANES] = grid[l, i, pl.ds(m * rows, rows), :]
        return carry

    lax.fori_loop(0, per, put, 0)
    for copy in halos + metas + bulks + smalls + copies + now.started + then.started:
        copy.wait_send()


def on_device(nt, ne, x, u, loc, cnt, val, err):
    per, levels, rows, width = x.shape
    lr = levels * rows
    members = per * ne
    slots = val.shape[1]
    col_count = width // ne
    vmem = pl.BlockSpec(memory_space=VMEM)
    dma = pltpu.SemaphoreType.DMA
    window = VMEM((WINDOW, ne, members, LANES), F32)
    whole = VMEM((width // LANES, per * lr, LANES), F32)
    return pl.pallas_call(
        functools.partial(cycle_kernel, nt, ne),
        out_shape=jax.ShapeDtypeStruct(x.shape, F32),
        in_specs=[vmem] * 6,
        out_specs=vmem,
        scratch_shapes=[
            window,
            window,
            VMEM((col_count // LANES, members * lr, LANES), F32),
            VMEM((WINDOW, BATCHES, 8, slots), F32),
            VMEM((levels, col_count // LANES, members * rows, LANES), F32),
            VMEM((levels, width // LANES, per * rows, LANES), F32),
            VMEM((2, per, levels, width), F32),
            VMEM((2, per, levels, width), F32),
            VMEM((lr, width), F32),
            VMEM((2, lr, width), F32),
            whole,
            VMEM((width // BLOCK, 3 * per * lr, BLOCK), BF16),
            VMEM((ne, 16, LANES), F32),
            VMEM((ne, 16, LANES), F32),
            VMEM((members, LANES), F32),
            VMEM((LANES, 3 * members), BF16),
            VMEM((WINDOW, levels, 3 * members, slots), BF16),
            VMEM((WINDOW, slots, 2 * members), BF16),
            VMEM((levels, rows * col_count, 3 * members), BF16),
            VMEM((lr * col_count, 2 * members), F32),
            VMEM((rows * col_count, BLOCK), F32),
            VMEM((lr * col_count, 2 * BLOCK), BF16),
            VMEM((LANES, 2 * members), F32),
            dma((2,)),
            dma((2,)),
            dma((4,)),
            dma((4,)),
            dma((ne,)),
            dma((ne,)),
            dma((ne,)),
            dma((ne,)),
            dma((EXCHANGE_SENDS,)),
            dma((WINDOW, ne)),
            dma((EXCHANGE_SENDS,)),
            dma((WINDOW, ne)),
            dma((levels, ne)),
            dma((levels, ne)),
            dma,
        ],
        compiler_params=pltpu.CompilerParams(collective_id=0, has_side_effects=True),
        name="cycle",
    )(x, u, loc, cnt.T, val, err)


def solution(mesh):
    in_specs = (
        P("ens", None, "tile", None),
        P(None, None, "tile", None),
        P(None, None, "tile"),
        P(None, "tile"),
        P(None, "tile"),
        P(None, "tile"),
    )
    out_specs = P("ens", None, "tile", None)
    body = functools.partial(on_device, mesh.shape["tile"], mesh.shape["ens"])
    return jax.shard_map(body, mesh=mesh, in_specs=in_specs, out_specs=out_specs, check_vma=False)
```

```python
import functools

import jax
import jax.numpy as jnp
from jax import lax
from jax.experimental import pallas as pl
from jax.experimental.pallas import tpu as pltpu
from jax.sharding import PartitionSpec as P

BATCHES = 2
REACH = 2
WINDOW = 2 * REACH + 1
SPREAD_RATE = 0.05
EPSILON = 1e-06
MESH = pl.DeviceIdType.MESH
VMEM = pltpu.VMEM
LANES = 128
BLOCK = 256
WIDE = 512
FORWARD_RIGHT = (2, 1, 3)
ORDER = (2, 1, 3, 0, 4)
F32 = jnp.float32
BF16 = jnp.bfloat16


def rdma(src, dst, send_sem, recv_sem, device):
    return pltpu.make_async_remote_copy(
        src_ref=src,
        dst_ref=dst,
        send_sem=send_sem,
        recv_sem=recv_sem,
        device_id=device,
        device_id_type=MESH,
    )


def greet(devices):
    barrier = pltpu.get_barrier_semaphore()
    for device in devices:
        pl.semaphore_signal(barrier, inc=1, device_id=device, device_id_type=MESH)
    return lambda: pl.semaphore_wait(barrier, len(devices))


def split2(value):
    high = value.astype(BF16).astype(F32)
    return high, value - high


class Exchange:
    def __init__(self, gathered, send, recv, t, e, nt, ne):
        self.gathered, self.send, self.recv = gathered, send, recv
        self.t, self.e, self.nt = t, e, nt
        self.right, self.left = lax.rem(e + 2, ne), lax.rem(e + ne - 2, ne)
        self.partner = e + 1 - 2 * lax.rem(e, 2)
        self.slots = [
            e,
            self.left,
            self.right,
            lax.rem(e + 4, ne),
            self.partner,
            lax.rem(self.partner + ne - 2, ne),
            lax.rem(self.partner + 2, ne),
            lax.rem(self.partner + 4, ne),
        ]
        self.started = []

    def go(self, k, rel, target_k, target_rel, device):
        copy = rdma(
            self.gathered.at[k, self.slots[rel]],
            self.gathered.at[target_k, self.slots[rel]],
            self.send.at[len(self.started)],
            self.recv.at[target_k, target_rel],
            device,
        )
        copy.start()
        self.started.append(copy)

    def arrive(self, k, rel):
        rdma(
            self.gathered.at[k, self.slots[rel]],
            self.gathered.at[k, self.slots[rel]],
            self.send.at[0],
            self.recv.at[k, rel],
            (self.t, self.partner),
        ).wait_recv()

    def along(self, k):
        self.go(k, 0, k, 1, (self.t, self.right))
        self.go(k, 0, k, 2, (self.t, self.left))
        self.go(k, 0, k, 4, (self.t, self.partner))

    def start(self):
        for offset in (1, -1, 2, -2):
            tile = lax.rem(self.t + self.nt + offset, self.nt)
            self.go(REACH, 0, REACH - offset, 0, (tile, self.e))
        self.along(REACH)

    def tiles(self, ks):
        for k in ks:
            self.arrive(k, 0)
            self.along(k)

    def sides(self, k):
        self.arrive(k, 1)
        if k in FORWARD_RIGHT:
            self.go(k, 1, k, 3, (self.t, self.right))
        self.go(k, 1, k, 5, (self.t, self.partner))
        self.arrive(k, 2)
        if k not in FORWARD_RIGHT:
            self.go(k, 2, k, 3, (self.t, self.left))
        self.go(k, 2, k, 6, (self.t, self.partner))

    def far(self, k):
        self.arrive(k, 3)
        self.go(k, 3, k, 7, (self.t, self.partner))

    def finish(self, k):
        for rel in (4, 5, 6, 7):
            self.arrive(k, rel)


EXCHANGE_SENDS = 4 + 3 * WINDOW + 3 * WINDOW + WINDOW


def tile_peers(t, e, nt):
    return [(lax.rem(t + nt + offset, nt), e) for offset in (1, -1, 2, -2)]


def ens_peers(t, e, ne):
    return [(t, lax.rem(e + d, ne)) for d in range(1, ne)]


def cycle_kernel(
    nt, ne,
    x_in, u_in, loc, cnt, val, err, out,
    x, u,
    first, later, cols, meta, leaving, grid,
    hs, hr, tmp, ub, bg, parts, sb, rb, second, x2,
    weights, shifts, states, total, closes, gains, ahead,
    halo_s, halo_r, meta_s, meta_r, bulk_s, bulk_r, small_s, small_r,
    first_s, first_r, later_s, later_r, out_s, out_r, own_sem, in_sem,
):
    t, e = lax.axis_index("tile"), lax.axis_index("ens")
    per, levels, rows, width = x.shape
    lr = levels * rows
    col_count = width // ne
    slots = loc.shape[2]

    inputs = [
        pltpu.make_async_copy(x_in, x, in_sem.at[0]),
        pltpu.make_async_copy(u_in, u, in_sem.at[1]),
    ]
    for copy in inputs:
        copy.start()
    all_here = greet(tile_peers(t, e, nt) + ens_peers(t, e, ne))
    slot_index = lax.broadcasted_iota(jnp.int32, (1, slots), 1)
    for b in range(BATCHES):
        for i in range(3):
            meta[REACH, b, i : i + 1, :] = loc[i, b : b + 1, :].astype(F32)
        meta[REACH, b, 3:4, :] = val[b : b + 1, :]
        meta[REACH, b, 4:5, :] = err[b : b + 1, :]
        meta[REACH, b, 5:6, :] = (slot_index < cnt[0:1, b : b + 1]).astype(F32)
        meta[REACH, b, 6:8, :] = jnp.zeros((2, slots), F32)
    for copy in inputs:
        copy.wait()

    def fill(m, carry):
        for l in range(levels):
            hs[0, m, l : l + 1, :] = x[m, l, 0:1, :]
            hs[1, m, l : l + 1, :] = x[m, l, rows - 1 : rows, :]
        return carry

    lax.fori_loop(0, per, fill, 0)
    all_here()
    up_tile, down_tile = lax.rem(t + nt - 1, nt), lax.rem(t + 1, nt)
    halos = [
        rdma(hs.at[1], hr.at[0], halo_s.at[0], halo_r.at[0], (down_tile, e)),
        rdma(hs.at[0], hr.at[1], halo_s.at[1], halo_r.at[1], (up_tile, e)),
    ]
    for copy in halos:
        copy.start()
    metas = []
    for i, offset in enumerate((1, -1, 2, -2)):
        copy = rdma(
            meta.at[REACH],
            meta.at[REACH - offset],
            meta_s.at[i],
            meta_r.at[i],
            (lax.rem(t + nt + offset, nt), e),
        )
        copy.start()
        metas.append(copy)
    for a in range(2):
        for l in range(levels):
            ub[a, l * rows : (l + 1) * rows, :] = u[a, l]
    for copy in halos:
        copy.wait_recv()
    has_up = jnp.where(t > 0, 1.0, 0.0).astype(F32)
    has_down = jnp.where(t < nt - 1, 1.0, 0.0).astype(F32)

    def step(m, carry):
        for l in range(levels):
            tmp[l * rows : (l + 1) * rows, :] = x[m, l]
        c = tmp[...]
        above = hr[0, m] * has_up
        below = hr[1, m] * has_down
        row = lax.broadcasted_iota(jnp.int32, (lr, width), 0)
        col = lax.broadcasted_iota(jnp.int32, (lr, width), 1)
        up = pltpu.roll(c, 1, 0)
        down = pltpu.roll(c, lr - 1, 0)
        for l in range(levels):
            up = jnp.where(row == l * rows, above[l : l + 1], up)
            down = jnp.where(row == l * rows + rows - 1, below[l : l + 1], down)
        west = jnp.where(col == 0, 0.0, pltpu.roll(c, 1, 1))
        east = jnp.where(col == width - 1, 0.0, pltpu.roll(c, width - 1, 1))
        wr, wc = ub[0], ub[1]
        tendency = (
            jnp.maximum(wr, 0.0) * (c - up)
            + jnp.minimum(wr, 0.0) * (down - c)
            + jnp.maximum(wc, 0.0) * (c - west)
            + jnp.minimum(wc, 0.0) * (east - c)
        )
        value = c - tendency + SPREAD_RATE * (up + down + west + east - 4.0 * c)
        for i in range(width // LANES):
            bg[i, pl.ds(m * lr, lr), :] = value[:, i * LANES : (i + 1) * LANES]
        return carry

    lax.fori_loop(0, per, step, 0)

    pieces = col_count // LANES

    def block_of(device):
        return pl.ds(device * pieces, pieces)

    def members_of(device):
        return pl.ds(pl.multiple_of(device * per * lr, per * lr), per * lr)

    bulks = []

    def send_bulk(d):
        peer = lax.rem(e + d, ne)
        copy = rdma(
            bg.at[block_of(peer)],
            cols.at[:, members_of(e)],
            bulk_s.at[d],
            bulk_r.at[d],
            (t, peer),
        )
        copy.start()
        bulks.append(copy)

    own = pltpu.make_async_copy(bg.at[block_of(e)], cols.at[:, members_of(e)], own_sem)
    own.start()
    for d in (1, 2, ne - 1, ne - 2):
        send_bulk(d)

    def split(kk, carry):
        f = jnp.concatenate([bg[2 * kk], bg[2 * kk + 1]], axis=1)
        high, rest = split2(f)
        middle, low = split2(rest)
        parts[kk] = jnp.concatenate([high, middle, low], axis=0).astype(BF16)
        return carry

    lax.fori_loop(0, width // BLOCK, split, 0)
    held = per * lr
    def pick(b, j):
        here = slice(j * BLOCK, (j + 1) * BLOCK)
        place = loc[2, b : b + 1, here] * rows + (loc[0, b : b + 1, here] - t * rows)
        column = loc[1, b : b + 1, here]
        down = lax.broadcasted_iota(jnp.int32, (BLOCK, BLOCK), 0)
        picked = jnp.zeros((3 * held, BLOCK), F32)
        for kk in range(x.shape[3] // BLOCK):
            hot = jnp.where(down == column - kk * BLOCK, 1.0, 0.0).astype(BF16)
            picked += jnp.dot(parts[kk], hot, preferred_element_type=F32)
        value = picked[0:held] + picked[held : 2 * held] + picked[2 * held :]
        mine = lax.broadcasted_iota(jnp.int32, (lr, BLOCK), 0) == place
        value = jnp.where(mine[None], value.reshape(per, lr, BLOCK), 0.0)
        value = jnp.sum(value, axis=1)
        for half in range(BLOCK // LANES):
            i = j * (BLOCK // LANES) + half
            part = value[:, half * LANES : (half + 1) * LANES]
            if b == 0:
                first[REACH, e, i * per : (i + 1) * per, :] = part
            else:
                sb[i, 0:per, :] = part

    members = per * ne
    halves = pieces
    width = col_count
    span = rows * width
    slot_blocks = slots // BLOCK
    exchanges = [
        Exchange(first, first_s, first_r, t, e, nt, ne),
        Exchange(later, later_s, later_r, t, e, nt, ne),
    ]
    inverse_col = 1.0 / float(x.shape[3] // 2)
    inverse_row = 1.0 / float(REACH * rows)

    def prior_of(k, batch, s):
        if batch:
            return jnp.concatenate([later[k, 2 * s], later[k, 2 * s + 1]], axis=1)
        return jnp.concatenate(
            [
                jnp.concatenate(
                    [first[k, d, i * per : (i + 1) * per, :] for d in range(ne)], axis=0
                )
                for i in (2 * s, 2 * s + 1)
            ],
            axis=1,
        )

    def prepare(k, batch):
        for s in range(slot_blocks):
            here = slice(s * BLOCK, (s + 1) * BLOCK)
            p = prior_of(k, batch, s)
            lev = meta[k, batch, 2:3, here]
            value = meta[k, batch, 3:4, here]
            error = meta[k, batch, 4:5, here]
            live = meta[k, batch, 5:6, here]
            average = jnp.sum(p, axis=0, keepdims=True) / members
            deviation = p - average
            variance = (
                jnp.sum(deviation * deviation, axis=0, keepdims=True) / (members - 1) + EPSILON
            )
            combined = variance + error
            shrink = jnp.sqrt(error / combined)
            mean_post = (error * average + variance * value) / combined
            shift = live * ((shrink - 1.0) * deviation + (mean_post - average))
            weight = deviation * (live / ((members - 1) * variance))
            high, low = split2(weight)
            for l in range(levels):
                factor = jnp.where(lev == float(l), 1.0, 0.5)
                scaled = (high * factor).astype(BF16)
                weights[k, l, 0:members, here] = scaled
                weights[k, l, members : 2 * members, here] = scaled
                weights[k, l, 2 * members : 3 * members, here] = (low * factor).astype(BF16)
            both = jnp.concatenate(split2(shift), axis=0)
            shifts[k, here, :] = both.T.astype(BF16)

    def cell_major(value):
        high, low = split2(value)
        return jnp.concatenate([high, low, high], axis=0).T.astype(BF16)

    def member_major(value):
        turned = value.T
        return turned[0:members] + turned[members : 2 * members]

    def load_states():
        for i in range(lr):
            here = pl.ds(i, members, stride=lr)
            value = jnp.concatenate([cols[h, here, :] for h in range(halves)], axis=1)
            states[i // rows, i % rows * width : (i % rows + 1) * width, :] = cell_major(value)
        total[...] = jnp.zeros_like(total)

    def part_of(device):
        return pl.ds(pl.multiple_of(device * per * rows, per * rows), per * rows)

    def store_states():
        for i in range(lr):
            here = pl.ds(i, members, stride=lr)
            change = member_major(total[i * width : (i + 1) * width, :])
            for h in range(halves):
                cols[h, here, :] = cols[h, here, :] + change[:, h * LANES : (h + 1) * LANES]

    def split_gain(gain):
        high = gain.astype(BF16)
        low = (gain - high.astype(F32)).astype(BF16)
        return jnp.concatenate([high, low], axis=1)

    def doubled(k, here):
        right = shifts[k, here, :]
        return jnp.concatenate([right, right], axis=0)

    def look(k):
        mine = pl.ds(pl.multiple_of(e * LANES, LANES), LANES)
        places = meta[REACH, 1, :, mine].T
        cell_row, cell_col, cell_lev = places[:, 0:1], places[:, 1:2], places[:, 2:3]

        def block(j, inner):
            here = pl.ds(pl.multiple_of(j * BLOCK, BLOCK), BLOCK)
            row_gap = (cell_row - meta[k, 0, 0:1, here]) * inverse_row
            col_gap = (cell_col - meta[k, 0, 1:2, here]) * inverse_col
            close = jnp.maximum(1.0 - row_gap * row_gap - col_gap * col_gap, 0.0)
            factor = jnp.where(meta[k, 0, 2:3, here] == 0.0, 0.5, 2.0)
            factor = jnp.where(cell_lev == 0.0, 1.0, factor)
            gain = jnp.dot(x2[...], weights[k, 0, :, here], preferred_element_type=F32)
            gain = gain * (close * close * factor)
            ahead[...] += jnp.dot(split_gain(gain), doubled(k, here), preferred_element_type=F32)
            return inner

        lax.fori_loop(0, slot_blocks, block, 0)

    def update(ks, batch, chosen=(0, 1), start=0, stop=None):
        first_cell = 1 if ks[0] == 2 * REACH else 0
        last_cell = rows - 1 if ks[0] == 0 else rows
        from_cell, to_cell = first_cell * width, last_cell * width
        steps = slots // WIDE
        stop = steps * len(ks) if stop is None else stop

        def block(i, inner):
            k = ks[0] if len(ks) == 1 else ks[0] + (ks[1] - ks[0]) * (i // steps)
            here = pl.ds(pl.multiple_of(i % steps * WIDE, WIDE), WIDE)
            cell_col = (
                lax.broadcasted_iota(jnp.int32, (width, WIDE), 0) + e * width
            ).astype(F32) * inverse_col
            col_gap = cell_col - meta[k, batch, 1:2, here] * inverse_col
            col_part = col_gap * col_gap
            obs_row = meta[k, batch, 0:1, here]
            for r in range(first_cell, last_cell):
                row_gap = ((t * rows + r).astype(F32) - obs_row) * inverse_row
                close = jnp.maximum((1.0 - row_gap * row_gap) - col_part, 0.0)
                closes[r * width : (r + 1) * width, :] = close * close
            right = doubled(k, here)
            for l in chosen:
                covariance = jnp.dot(
                    states[l, from_cell:to_cell, :],
                    weights[k, l, :, here],
                    preferred_element_type=F32,
                )
                mine = slice(l * span + from_cell, l * span + to_cell)
                gains[mine, :] = split_gain(covariance * closes[from_cell:to_cell, :])
                total[mine, :] += jnp.dot(gains[mine, :], right, preferred_element_type=F32)
            return inner

        lax.fori_loop(start, stop, block, 0)

    now, then = exchanges
    for j in range(slot_blocks):
        pick(0, j)
    now.start()
    for d in (4, 3, 5):
        send_bulk(d)
    for j in range(slot_blocks):
        pick(1, j)
    smalls = []
    for d in (4, 3, 5, 2, 6, 1, 7):
        peer = lax.rem(e + d, ne)
        copy = rdma(sb.at[peer], rb.at[e], small_s.at[d], small_r.at[d], (t, peer))
        copy.start()
        smalls.append(copy)
    rb[e] = sb[e]
    now.tiles((1, 3))
    now.sides(2)
    now.tiles((0, 4))
    for d in range(1, ne):
        source = lax.rem(e + ne - d, ne)
        rdma(
            sb.at[source], rb.at[source], small_s.at[d], small_r.at[d], (t, source)
        ).wait_recv()
    for s in range(ne):
        second[s * per : (s + 1) * per, :] = rb[s, 0:per, :]
    x2[...] = cell_major(second[...])
    ahead[...] = jnp.zeros_like(ahead)
    now.far(2)
    own.wait()
    for d in range(1, ne):
        source = lax.rem(e + ne - d, ne)
        rdma(
            bg.at[block_of(source)],
            cols.at[:, members_of(source)],
            bulk_s.at[d],
            bulk_r.at[d],
            (t, source),
        ).wait_recv()
    for i, offset in enumerate((1, -1, 2, -2)):
        rdma(
            meta.at[REACH],
            meta.at[REACH - offset],
            meta_s.at[i],
            meta_r.at[i],
            (up_tile, e),
        ).wait_recv()
    load_states()
    now.finish(2)
    prepare(2, 0)
    look(2)
    update((2,), 0, stop=1)
    now.sides(1)
    now.sides(3)
    update((2,), 0, start=1)
    now.far(1)
    now.far(3)
    now.sides(0)
    now.sides(4)
    now.finish(1)
    prepare(1, 0)
    look(1)
    now.far(0)
    now.far(4)
    for k in (3, 0, 4):
        now.finish(k)
        prepare(k, 0)
        look(k)
    later[REACH, e] = second[...] + member_major(ahead[...])
    then.start()
    update((1,), 0)
    then.tiles((1, 3, 0, 4))
    then.sides(2)
    update((3,), 0)
    then.far(2)
    then.sides(1)
    then.sides(3)
    update((0,), 0)
    then.sides(0)
    then.sides(4)
    then.far(1)
    then.far(3)
    update((4,), 0)
    then.far(0)
    then.far(4)
    store_states()
    load_states()
    then.finish(2)
    prepare(2, 1)
    update((2,), 1)
    for k in (1, 3):
        then.finish(k)
        prepare(k, 1)
    update((1, 3), 1)
    for k in (0, 4):
        then.finish(k)
        prepare(k, 1)
    copies, homes = [], []
    for l in range(levels):
        update((0,), 1, chosen=(l,))
        update((4,), 1, chosen=(l,))
        for r in range(rows):
            change = member_major(total[(l * rows + r) * width : (l * rows + r + 1) * width, :])
            for h in range(halves):
                leaving[l, h, pl.ds(r, members, stride=rows), :] = (
                    cols[h, pl.ds(l * rows + r, members, stride=lr), :]
                    + change[:, h * LANES : (h + 1) * LANES]
                )
        for d in (4, 3, 5, 2, 6, 1, 7):
            peer = lax.rem(e + d, ne)
            copy = rdma(
                leaving.at[l, :, part_of(peer)],
                grid.at[l, block_of(e)],
                out_s.at[l, d],
                out_r.at[l, d],
                (t, peer),
            )
            copy.start()
            copies.append(copy)
        home = pltpu.make_async_copy(
            leaving.at[l, :, part_of(e)], grid.at[l, block_of(e)], out_s.at[l, 0]
        )
        home.start()
        homes.append(home)
    for l in range(levels):
        homes[l].wait()
        for d in range(1, ne):
            source = lax.rem(e + ne - d, ne)
            rdma(
                leaving.at[l, :, part_of(source)],
                grid.at[l, block_of(source)],
                out_s.at[l, d],
                out_r.at[l, d],
                (t, source),
            ).wait_recv()

    def put(m, carry):
        for l in range(levels):
            for i in range(x.shape[3] // LANES):
                out[m, l, :, i * LANES : (i + 1) * LANES] = grid[l, i, pl.ds(m * rows, rows), :]
        return carry

    lax.fori_loop(0, per, put, 0)
    for copy in halos + metas + bulks + smalls + copies + now.started + then.started:
        copy.wait_send()


def on_device(nt, ne, x, u, loc, cnt, val, err):
    per, levels, rows, width = x.shape
    lr = levels * rows
    members = per * ne
    slots = val.shape[1]
    col_count = width // ne
    vmem = pl.BlockSpec(memory_space=VMEM)
    dma = pltpu.SemaphoreType.DMA
    window = VMEM((WINDOW, ne, members, LANES), F32)
    whole = VMEM((width // LANES, per * lr, LANES), F32)
    return pl.pallas_call(
        functools.partial(cycle_kernel, nt, ne),
        out_shape=jax.ShapeDtypeStruct(x.shape, F32),
        in_specs=[pl.BlockSpec(memory_space=pl.ANY)] * 2 + [vmem] * 4,
        out_specs=vmem,
        scratch_shapes=[
            VMEM(x.shape, F32),
            VMEM(u.shape, F32),
            window,
            window,
            VMEM((col_count // LANES, members * lr, LANES), F32),
            VMEM((WINDOW, BATCHES, 8, slots), F32),
            VMEM((levels, col_count // LANES, members * rows, LANES), F32),
            VMEM((levels, width // LANES, per * rows, LANES), F32),
            VMEM((2, per, levels, width), F32),
            VMEM((2, per, levels, width), F32),
            VMEM((lr, width), F32),
            VMEM((2, lr, width), F32),
            whole,
            VMEM((width // BLOCK, 3 * per * lr, BLOCK), BF16),
            VMEM((ne, 16, LANES), F32),
            VMEM((ne, 16, LANES), F32),
            VMEM((members, LANES), F32),
            VMEM((LANES, 3 * members), BF16),
            VMEM((WINDOW, levels, 3 * members, slots), BF16),
            VMEM((WINDOW, slots, 2 * members), BF16),
            VMEM((levels, rows * col_count, 3 * members), BF16),
            VMEM((lr * col_count, 2 * members), F32),
            VMEM((rows * col_count, WIDE), F32),
            VMEM((lr * col_count, 2 * WIDE), BF16),
            VMEM((LANES, 2 * members), F32),
            dma((2,)),
            dma((2,)),
            dma((4,)),
            dma((4,)),
            dma((ne,)),
            dma((ne,)),
            dma((ne,)),
            dma((ne,)),
            dma((EXCHANGE_SENDS,)),
            dma((WINDOW, ne)),
            dma((EXCHANGE_SENDS,)),
            dma((WINDOW, ne)),
            dma((levels, ne)),
            dma((levels, ne)),
            dma,
            dma((2,)),
        ],
        compiler_params=pltpu.CompilerParams(collective_id=0, has_side_effects=True),
        name="cycle",
    )(x, u, loc, cnt.T, val, err)


def solution(mesh):
    in_specs = (
        P("ens", None, "tile", None),
        P(None, None, "tile", None),
        P(None, None, "tile"),
        P(None, "tile"),
        P(None, "tile"),
        P(None, "tile"),
    )
    out_specs = P("ens", None, "tile", None)
    body = functools.partial(on_device, mesh.shape["tile"], mesh.shape["ens"])
    return jax.shard_map(body, mesh=mesh, in_specs=in_specs, out_specs=out_specs, check_vma=False)
```

```python
import functools

import jax
import jax.numpy as jnp
from jax import lax
from jax.experimental import pallas as pl
from jax.experimental.pallas import tpu as pltpu
from jax.sharding import PartitionSpec as P

BATCHES = 2
REACH = 2
WINDOW = 2 * REACH + 1
SPREAD_RATE = 0.05
EPSILON = 1e-06
MESH = pl.DeviceIdType.MESH
VMEM = pltpu.VMEM
LANES = 128
BLOCK = 256
WIDE = 512
FORWARD_RIGHT = (2, 1, 3)
ORDER = (2, 1, 3, 0, 4)
F32 = jnp.float32
BF16 = jnp.bfloat16


def rdma(src, dst, send_sem, recv_sem, device):
    return pltpu.make_async_remote_copy(
        src_ref=src,
        dst_ref=dst,
        send_sem=send_sem,
        recv_sem=recv_sem,
        device_id=device,
        device_id_type=MESH,
    )


def greet(devices):
    barrier = pltpu.get_barrier_semaphore()
    for device in devices:
        pl.semaphore_signal(barrier, inc=1, device_id=device, device_id_type=MESH)
    return lambda: pl.semaphore_wait(barrier, len(devices))


def split2(value):
    high = value.astype(BF16).astype(F32)
    return high, value - high


class Exchange:
    def __init__(self, gathered, send, recv, t, e, nt, ne):
        self.gathered, self.send, self.recv = gathered, send, recv
        self.t, self.e, self.nt = t, e, nt
        self.right, self.left = lax.rem(e + 2, ne), lax.rem(e + ne - 2, ne)
        self.partner = e + 1 - 2 * lax.rem(e, 2)
        self.slots = [
            e,
            self.left,
            self.right,
            lax.rem(e + 4, ne),
            self.partner,
            lax.rem(self.partner + ne - 2, ne),
            lax.rem(self.partner + 2, ne),
            lax.rem(self.partner + 4, ne),
        ]
        self.started = []

    def go(self, k, rel, target_k, target_rel, device):
        copy = rdma(
            self.gathered.at[k, self.slots[rel]],
            self.gathered.at[target_k, self.slots[rel]],
            self.send.at[len(self.started)],
            self.recv.at[target_k, target_rel],
            device,
        )
        copy.start()
        self.started.append(copy)

    def arrive(self, k, rel):
        rdma(
            self.gathered.at[k, self.slots[rel]],
            self.gathered.at[k, self.slots[rel]],
            self.send.at[0],
            self.recv.at[k, rel],
            (self.t, self.partner),
        ).wait_recv()

    def along(self, k):
        self.go(k, 0, k, 1, (self.t, self.right))
        self.go(k, 0, k, 2, (self.t, self.left))
        self.go(k, 0, k, 4, (self.t, self.partner))

    def start(self):
        for offset in (1, -1, 2, -2):
            tile = lax.rem(self.t + self.nt + offset, self.nt)
            self.go(REACH, 0, REACH - offset, 0, (tile, self.e))
        self.along(REACH)

    def tiles(self, ks):
        for k in ks:
            self.arrive(k, 0)
            self.along(k)

    def sides(self, k):
        self.arrive(k, 1)
        if k in FORWARD_RIGHT:
            self.go(k, 1, k, 3, (self.t, self.right))
        self.go(k, 1, k, 5, (self.t, self.partner))
        self.arrive(k, 2)
        if k not in FORWARD_RIGHT:
            self.go(k, 2, k, 3, (self.t, self.left))
        self.go(k, 2, k, 6, (self.t, self.partner))

    def far(self, k):
        self.arrive(k, 3)
        self.go(k, 3, k, 7, (self.t, self.partner))

    def finish(self, k):
        for rel in (4, 5, 6, 7):
            self.arrive(k, rel)


EXCHANGE_SENDS = 4 + 3 * WINDOW + 3 * WINDOW + WINDOW


def tile_peers(t, e, nt):
    return [(lax.rem(t + nt + offset, nt), e) for offset in (1, -1, 2, -2)]


def ens_peers(t, e, ne):
    return [(t, lax.rem(e + d, ne)) for d in range(1, ne)]


def cycle_kernel(
    nt, ne,
    x_in, u_in, loc, cnt, val, err, out,
    x, u,
    first, later, cols, meta, leaving, grid,
    hs, hr, tmp, ub, bg, parts, sb, rb, second, x2,
    weights, shifts, states, total, closes, gains, ahead,
    halo_s, halo_r, meta_s, meta_r, bulk_s, bulk_r, small_s, small_r,
    first_s, first_r, later_s, later_r, out_s, out_r, own_sem, in_sem,
):
    t, e = lax.axis_index("tile"), lax.axis_index("ens")
    per, levels, rows, width = x.shape
    lr = levels * rows
    col_count = width // ne
    slots = loc.shape[2]

    inputs = [
        pltpu.make_async_copy(x_in, x, in_sem.at[0]),
        pltpu.make_async_copy(u_in, u, in_sem.at[1]),
    ]
    for copy in inputs:
        copy.start()
    all_here = greet(tile_peers(t, e, nt) + ens_peers(t, e, ne))
    slot_index = lax.broadcasted_iota(jnp.int32, (1, slots), 1)
    for b in range(BATCHES):
        for i in range(3):
            meta[REACH, b, i : i + 1, :] = loc[i, b : b + 1, :].astype(F32)
        meta[REACH, b, 3:4, :] = val[b : b + 1, :]
        meta[REACH, b, 4:5, :] = err[b : b + 1, :]
        meta[REACH, b, 5:6, :] = (slot_index < cnt[0:1, b : b + 1]).astype(F32)
        meta[REACH, b, 6:8, :] = jnp.zeros((2, slots), F32)
    for copy in inputs:
        copy.wait()

    def fill(m, carry):
        for l in range(levels):
            hs[0, m, l : l + 1, :] = x[m, l, 0:1, :]
            hs[1, m, l : l + 1, :] = x[m, l, rows - 1 : rows, :]
        return carry

    lax.fori_loop(0, per, fill, 0)
    all_here()
    up_tile, down_tile = lax.rem(t + nt - 1, nt), lax.rem(t + 1, nt)
    halos = [
        rdma(hs.at[1], hr.at[0], halo_s.at[0], halo_r.at[0], (down_tile, e)),
        rdma(hs.at[0], hr.at[1], halo_s.at[1], halo_r.at[1], (up_tile, e)),
    ]
    for copy in halos:
        copy.start()
    metas = []
    for i, offset in enumerate((1, -1, 2, -2)):
        copy = rdma(
            meta.at[REACH],
            meta.at[REACH - offset],
            meta_s.at[i],
            meta_r.at[i],
            (lax.rem(t + nt + offset, nt), e),
        )
        copy.start()
        metas.append(copy)
    for a in range(2):
        for l in range(levels):
            ub[a, l * rows : (l + 1) * rows, :] = u[a, l]
    for copy in halos:
        copy.wait_recv()
    has_up = jnp.where(t > 0, 1.0, 0.0).astype(F32)
    has_down = jnp.where(t < nt - 1, 1.0, 0.0).astype(F32)

    def step(m, carry):
        for l in range(levels):
            tmp[l * rows : (l + 1) * rows, :] = x[m, l]
        c = tmp[...]
        above = hr[0, m] * has_up
        below = hr[1, m] * has_down
        row = lax.broadcasted_iota(jnp.int32, (lr, width), 0)
        col = lax.broadcasted_iota(jnp.int32, (lr, width), 1)
        up = pltpu.roll(c, 1, 0)
        down = pltpu.roll(c, lr - 1, 0)
        for l in range(levels):
            up = jnp.where(row == l * rows, above[l : l + 1], up)
            down = jnp.where(row == l * rows + rows - 1, below[l : l + 1], down)
        west = jnp.where(col == 0, 0.0, pltpu.roll(c, 1, 1))
        east = jnp.where(col == width - 1, 0.0, pltpu.roll(c, width - 1, 1))
        wr, wc = ub[0], ub[1]
        tendency = (
            jnp.maximum(wr, 0.0) * (c - up)
            + jnp.minimum(wr, 0.0) * (down - c)
            + jnp.maximum(wc, 0.0) * (c - west)
            + jnp.minimum(wc, 0.0) * (east - c)
        )
        value = c - tendency + SPREAD_RATE * (up + down + west + east - 4.0 * c)
        for i in range(width // LANES):
            bg[i, pl.ds(m * lr, lr), :] = value[:, i * LANES : (i + 1) * LANES]
        return carry

    lax.fori_loop(0, per, step, 0)

    pieces = col_count // LANES

    def block_of(device):
        return pl.ds(device * pieces, pieces)

    def members_of(device):
        return pl.ds(pl.multiple_of(device * per * lr, per * lr), per * lr)

    bulks = []

    def send_bulk(d):
        peer = lax.rem(e + d, ne)
        copy = rdma(
            bg.at[block_of(peer)],
            cols.at[:, members_of(e)],
            bulk_s.at[d],
            bulk_r.at[d],
            (t, peer),
        )
        copy.start()
        bulks.append(copy)

    own = pltpu.make_async_copy(bg.at[block_of(e)], cols.at[:, members_of(e)], own_sem)
    own.start()
    for d in (1, 2, ne - 1, ne - 2):
        send_bulk(d)

    def split(kk, carry):
        f = jnp.concatenate([bg[2 * kk], bg[2 * kk + 1]], axis=1)
        high, rest = split2(f)
        middle, low = split2(rest)
        parts[kk] = jnp.concatenate([high, middle, low], axis=0).astype(BF16)
        return carry

    lax.fori_loop(0, width // BLOCK, split, 0)
    held = per * lr
    def pick(b, j):
        here = slice(j * BLOCK, (j + 1) * BLOCK)
        place = loc[2, b : b + 1, here] * rows + (loc[0, b : b + 1, here] - t * rows)
        column = loc[1, b : b + 1, here]
        down = lax.broadcasted_iota(jnp.int32, (BLOCK, BLOCK), 0)
        picked = jnp.zeros((3 * held, BLOCK), F32)
        for kk in range(x.shape[3] // BLOCK):
            hot = jnp.where(down == column - kk * BLOCK, 1.0, 0.0).astype(BF16)
            picked += jnp.dot(parts[kk], hot, preferred_element_type=F32)
        value = picked[0:held] + picked[held : 2 * held] + picked[2 * held :]
        mine = lax.broadcasted_iota(jnp.int32, (lr, BLOCK), 0) == place
        value = jnp.where(mine[None], value.reshape(per, lr, BLOCK), 0.0)
        value = jnp.sum(value, axis=1)
        for half in range(BLOCK // LANES):
            i = j * (BLOCK // LANES) + half
            part = value[:, half * LANES : (half + 1) * LANES]
            if b == 0:
                first[REACH, e, i * per : (i + 1) * per, :] = part
            else:
                sb[i, 0:per, :] = part

    members = per * ne
    halves = pieces
    width = col_count
    span = rows * width
    slot_blocks = slots // BLOCK
    exchanges = [
        Exchange(first, first_s, first_r, t, e, nt, ne),
        Exchange(later, later_s, later_r, t, e, nt, ne),
    ]
    inverse_col = 1.0 / float(x.shape[3] // 2)
    inverse_row = 1.0 / float(REACH * rows)

    def prior_of(k, batch, s):
        if batch:
            return jnp.concatenate([later[k, 2 * s], later[k, 2 * s + 1]], axis=1)
        return jnp.concatenate(
            [
                jnp.concatenate(
                    [first[k, d, i * per : (i + 1) * per, :] for d in range(ne)], axis=0
                )
                for i in (2 * s, 2 * s + 1)
            ],
            axis=1,
        )

    def prepare(k, batch):
        for s in range(slot_blocks):
            here = slice(s * BLOCK, (s + 1) * BLOCK)
            p = prior_of(k, batch, s)
            lev = meta[k, batch, 2:3, here]
            value = meta[k, batch, 3:4, here]
            error = meta[k, batch, 4:5, here]
            live = meta[k, batch, 5:6, here]
            average = jnp.sum(p, axis=0, keepdims=True) / members
            deviation = p - average
            variance = (
                jnp.sum(deviation * deviation, axis=0, keepdims=True) / (members - 1) + EPSILON
            )
            combined = variance + error
            shrink = jnp.sqrt(error / combined)
            mean_post = (error * average + variance * value) / combined
            shift = live * ((shrink - 1.0) * deviation + (mean_post - average))
            weight = deviation * (live / ((members - 1) * variance))
            high, low = split2(weight)
            factor = jnp.where(lev == 0.0, 1.0, 0.5)
            scaled = (high * factor).astype(BF16)
            weights[k, 0:members, here] = scaled
            weights[k, members : 2 * members, here] = scaled
            weights[k, 2 * members : 3 * members, here] = (low * factor).astype(BF16)
            both = jnp.concatenate(split2(shift), axis=0)
            shifts[k, here, :] = both.T.astype(BF16)

    def cell_major(value):
        high, low = split2(value)
        return jnp.concatenate([high, low, high], axis=0).T.astype(BF16)

    def member_major(value):
        turned = value.T
        return turned[0:members] + turned[members : 2 * members]

    def load_states():
        for i in range(lr):
            here = pl.ds(i, members, stride=lr)
            value = jnp.concatenate([cols[h, here, :] for h in range(halves)], axis=1)
            states[i // rows, i % rows * width : (i % rows + 1) * width, :] = cell_major(value)
        total[...] = jnp.zeros_like(total)

    def part_of(device):
        return pl.ds(pl.multiple_of(device * per * rows, per * rows), per * rows)

    def store_states():
        for i in range(lr):
            here = pl.ds(i, members, stride=lr)
            change = member_major(total[i * width : (i + 1) * width, :])
            for h in range(halves):
                cols[h, here, :] = cols[h, here, :] + change[:, h * LANES : (h + 1) * LANES]

    def split_gain(gain):
        high = gain.astype(BF16)
        low = (gain - high.astype(F32)).astype(BF16)
        return jnp.concatenate([high, low], axis=1)

    def doubled(k, here):
        right = shifts[k, here, :]
        return jnp.concatenate([right, right], axis=0)

    def look(k):
        mine = pl.ds(pl.multiple_of(e * LANES, LANES), LANES)
        places = meta[REACH, 1, :, mine].T
        cell_row, cell_col, cell_lev = places[:, 0:1], places[:, 1:2], places[:, 2:3]

        def block(j, inner):
            here = pl.ds(pl.multiple_of(j * BLOCK, BLOCK), BLOCK)
            row_gap = (cell_row - meta[k, 0, 0:1, here]) * inverse_row
            col_gap = (cell_col - meta[k, 0, 1:2, here]) * inverse_col
            close = jnp.maximum(1.0 - row_gap * row_gap - col_gap * col_gap, 0.0)
            factor = jnp.where(meta[k, 0, 2:3, here] == 0.0, 0.5, 2.0)
            factor = jnp.where(cell_lev == 0.0, 1.0, factor)
            gain = jnp.dot(x2[...], weights[k, :, here], preferred_element_type=F32)
            gain = gain * (close * close * factor)
            ahead[...] += jnp.dot(split_gain(gain), doubled(k, here), preferred_element_type=F32)
            return inner

        lax.fori_loop(0, slot_blocks, block, 0)

    def update(ks, batch, chosen=(0, 1), start=0, stop=None):
        first_cell = 1 if ks[0] == 2 * REACH else 0
        last_cell = rows - 1 if ks[0] == 0 else rows
        from_cell, to_cell = first_cell * width, last_cell * width
        steps = slots // WIDE
        stop = steps * len(ks) if stop is None else stop

        def block(i, inner):
            k = ks[0] if len(ks) == 1 else ks[0] + (ks[1] - ks[0]) * (i // steps)
            here = pl.ds(pl.multiple_of(i % steps * WIDE, WIDE), WIDE)
            cell_col = (
                lax.broadcasted_iota(jnp.int32, (width, WIDE), 0) + e * width
            ).astype(F32) * inverse_col
            col_gap = cell_col - meta[k, batch, 1:2, here] * inverse_col
            col_part = col_gap * col_gap
            obs_row = meta[k, batch, 0:1, here]
            for r in range(first_cell, last_cell):
                row_gap = ((t * rows + r).astype(F32) - obs_row) * inverse_row
                close = jnp.maximum((1.0 - row_gap * row_gap) - col_part, 0.0)
                closes[r * width : (r + 1) * width, :] = close * close
            right = doubled(k, here)
            for l in chosen:
                covariance = jnp.dot(
                    states[l, from_cell:to_cell, :],
                    weights[k, :, here],
                    preferred_element_type=F32,
                )
                mine = slice(l * span + from_cell, l * span + to_cell)
                gain = covariance * closes[from_cell:to_cell, :]
                if l:
                    gain = gain * jnp.where(meta[k, batch, 2:3, here] == 0.0, 0.5, 2.0)
                gains[mine, :] = split_gain(gain)
                total[mine, :] += jnp.dot(gains[mine, :], right, preferred_element_type=F32)
            return inner

        lax.fori_loop(start, stop, block, 0)

    now, then = exchanges
    for j in range(slot_blocks):
        pick(0, j)
    now.start()
    for j in range(slot_blocks):
        pick(1, j)
    smalls = []
    for d in (4, 3, 5, 2, 6, 1, 7):
        peer = lax.rem(e + d, ne)
        copy = rdma(sb.at[peer], rb.at[e], small_s.at[d], small_r.at[d], (t, peer))
        copy.start()
        smalls.append(copy)
    rb[e] = sb[e]
    now.sides(2)
    for d in (4, 3, 5):
        send_bulk(d)
    now.tiles((1, 3))
    for d in range(1, ne):
        source = lax.rem(e + ne - d, ne)
        rdma(
            sb.at[source], rb.at[source], small_s.at[d], small_r.at[d], (t, source)
        ).wait_recv()
    for s in range(ne):
        second[s * per : (s + 1) * per, :] = rb[s, 0:per, :]
    x2[...] = cell_major(second[...])
    ahead[...] = jnp.zeros_like(ahead)
    now.far(2)
    now.tiles((0, 4))
    for i, offset in enumerate((1, -1, 2, -2)):
        rdma(
            meta.at[REACH],
            meta.at[REACH - offset],
            meta_s.at[i],
            meta_r.at[i],
            (up_tile, e),
        ).wait_recv()
    now.finish(2)
    prepare(2, 0)
    look(2)
    own.wait()
    for d in range(1, ne):
        source = lax.rem(e + ne - d, ne)
        rdma(
            bg.at[block_of(source)],
            cols.at[:, members_of(source)],
            bulk_s.at[d],
            bulk_r.at[d],
            (t, source),
        ).wait_recv()
    load_states()
    update((2,), 0, stop=1)
    now.sides(1)
    now.sides(3)
    update((2,), 0, start=1)
    now.far(1)
    now.far(3)
    now.sides(0)
    now.sides(4)
    now.finish(1)
    prepare(1, 0)
    look(1)
    now.far(0)
    now.far(4)
    for k in (3, 0, 4):
        now.finish(k)
        prepare(k, 0)
        look(k)
    later[REACH, e] = second[...] + member_major(ahead[...])
    then.start()
    update((1,), 0)
    then.tiles((1, 3, 0, 4))
    then.sides(2)
    update((3,), 0)
    then.far(2)
    then.sides(1)
    then.sides(3)
    update((0,), 0)
    then.sides(0)
    then.sides(4)
    then.far(1)
    then.far(3)
    update((4,), 0)
    then.far(0)
    then.far(4)
    store_states()
    load_states()
    then.finish(2)
    prepare(2, 1)
    update((2,), 1)
    for k in (1, 3):
        then.finish(k)
        prepare(k, 1)
    update((1, 3), 1)
    for k in (0, 4):
        then.finish(k)
        prepare(k, 1)
    copies, homes = [], []
    for l in range(levels):
        update((0,), 1, chosen=(l,))
        update((4,), 1, chosen=(l,))
        for r in range(rows):
            change = member_major(total[(l * rows + r) * width : (l * rows + r + 1) * width, :])
            for h in range(halves):
                leaving[l, h, pl.ds(r, members, stride=rows), :] = (
                    cols[h, pl.ds(l * rows + r, members, stride=lr), :]
                    + change[:, h * LANES : (h + 1) * LANES]
                )
        for d in (4, 3, 5, 2, 6, 1, 7):
            peer = lax.rem(e + d, ne)
            copy = rdma(
                leaving.at[l, :, part_of(peer)],
                grid.at[l, block_of(e)],
                out_s.at[l, d],
                out_r.at[l, d],
                (t, peer),
            )
            copy.start()
            copies.append(copy)
        home = pltpu.make_async_copy(
            leaving.at[l, :, part_of(e)], grid.at[l, block_of(e)], out_s.at[l, 0]
        )
        home.start()
        homes.append(home)
    for l in range(levels):
        homes[l].wait()
        for d in range(1, ne):
            source = lax.rem(e + ne - d, ne)
            rdma(
                leaving.at[l, :, part_of(source)],
                grid.at[l, block_of(source)],
                out_s.at[l, d],
                out_r.at[l, d],
                (t, source),
            ).wait_recv()

    def put(m, carry):
        for l in range(levels):
            for i in range(x.shape[3] // LANES):
                out[m, l, :, i * LANES : (i + 1) * LANES] = grid[l, i, pl.ds(m * rows, rows), :]
        return carry

    lax.fori_loop(0, per, put, 0)
    for copy in halos + metas + bulks + smalls + copies + now.started + then.started:
        copy.wait_send()


def on_device(nt, ne, x, u, loc, cnt, val, err):
    per, levels, rows, width = x.shape
    lr = levels * rows
    members = per * ne
    slots = val.shape[1]
    col_count = width // ne
    vmem = pl.BlockSpec(memory_space=VMEM)
    dma = pltpu.SemaphoreType.DMA
    window = VMEM((WINDOW, ne, members, LANES), F32)
    whole = VMEM((width // LANES, per * lr, LANES), F32)
    return pl.pallas_call(
        functools.partial(cycle_kernel, nt, ne),
        out_shape=jax.ShapeDtypeStruct(x.shape, F32),
        in_specs=[pl.BlockSpec(memory_space=pl.ANY)] * 2 + [vmem] * 4,
        out_specs=vmem,
        scratch_shapes=[
            VMEM(x.shape, F32),
            VMEM(u.shape, F32),
            window,
            window,
            VMEM((col_count // LANES, members * lr, LANES), F32),
            VMEM((WINDOW, BATCHES, 8, slots), F32),
            VMEM((levels, col_count // LANES, members * rows, LANES), F32),
            VMEM((levels, width // LANES, per * rows, LANES), F32),
            VMEM((2, per, levels, width), F32),
            VMEM((2, per, levels, width), F32),
            VMEM((lr, width), F32),
            VMEM((2, lr, width), F32),
            whole,
            VMEM((width // BLOCK, 3 * per * lr, BLOCK), BF16),
            VMEM((ne, 16, LANES), F32),
            VMEM((ne, 16, LANES), F32),
            VMEM((members, LANES), F32),
            VMEM((LANES, 3 * members), BF16),
            VMEM((WINDOW, 3 * members, slots), BF16),
            VMEM((WINDOW, slots, 2 * members), BF16),
            VMEM((levels, rows * col_count, 3 * members), BF16),
            VMEM((lr * col_count, 2 * members), F32),
            VMEM((rows * col_count, WIDE), F32),
            VMEM((lr * col_count, 2 * WIDE), BF16),
            VMEM((LANES, 2 * members), F32),
            dma((2,)),
            dma((2,)),
            dma((4,)),
            dma((4,)),
            dma((ne,)),
            dma((ne,)),
            dma((ne,)),
            dma((ne,)),
            dma((EXCHANGE_SENDS,)),
            dma((WINDOW, ne)),
            dma((EXCHANGE_SENDS,)),
            dma((WINDOW, ne)),
            dma((levels, ne)),
            dma((levels, ne)),
            dma,
            dma((2,)),
        ],
        compiler_params=pltpu.CompilerParams(collective_id=0, has_side_effects=True),
        name="cycle",
    )(x, u, loc, cnt.T, val, err)


def solution(mesh):
    in_specs = (
        P("ens", None, "tile", None),
        P(None, None, "tile", None),
        P(None, None, "tile"),
        P(None, "tile"),
        P(None, "tile"),
        P(None, "tile"),
    )
    out_specs = P("ens", None, "tile", None)
    body = functools.partial(on_device, mesh.shape["tile"], mesh.shape["ens"])
    return jax.shard_map(body, mesh=mesh, in_specs=in_specs, out_specs=out_specs, check_vma=False)
```
